128 devices in a mesh: dom: 16 (over x, y_lo, core), cls: 8 (over y_hi, z).
Axes of the slice: x: 4, y: 4 (y_hi: 2, y_lo: 2; y = y_hi * 2 + y_lo), z: 4, core: 2. Of those that a mesh axis runs over, the one named last changes fastest.
Arguments:
- particles: bfloat16 [256, 16640], P('dom'), may hold values from -5 to 5
- references: bfloat16 [16, 16, 16640], P('dom', 'cls'), may hold values from -0.15504342 to 0.15504342
- inv_noise: float32 [8320], replicated, may hold values from 0.3 to 3
- shifts: int32 [128, 2], replicated, may hold values from -5 to 5, as said below
- prior_class: int32 [256], P('dom'), may hold values from 0 to 15
- prior_orient: int32 [256], P('dom'), may hold values from 0 to 15
Outputs:
- back_projection: float32 [16, 16, 16640], P('dom', 'cls')
- class_weights: float32 [16, 16], P('dom', 'cls')
- log_norm: float32 [256], P('dom')
The draws below stay inside these ranges and needn't reach their ends.
Inputs may be any that keep to these rules, and one draw needn't show every extreme that they name: `shifts`: row 0 is the zero translation and row 1 is (5, -5).
All inputs are finite; a program needn't handle non-finite values.
Results may differ from the reference program's by a relative error of at most 0.0022.
Values may be sent and summed in bfloat16 or wider, within the bound.
A program may use at most 64 MiB of HBM per device.

```python
import math
import jax
import jax.numpy as jnp
from jax import lax

L = 128
PIX = 8320
FEAT = 16640
TRANS = 128
SHIFT_MAX = 5
ORI_DEV = 2
CLASSES = 16
ORIENT = 16
NPART = 256
N_CLS = 8


def shared_refs(key):
    spread = 6.0 / FEAT ** 0.5
    base = jnp.clip(jax.random.normal(jax.random.fold_in(key, 11), (CLASSES, ORIENT, FEAT), jnp.float32), -3.0, 3.0)
    return base * spread


def draw_references(key, part):
    return shared_refs(key).astype(jnp.bfloat16)


def draw_particles(key, part):
    noise = jnp.clip(jax.random.normal(jax.random.fold_in(key, 12), (NPART, FEAT), jnp.float32), -5.0, 5.0)
    flat_refs = shared_refs(key).reshape(CLASSES * ORIENT, FEAT)
    picked = jax.random.randint(jax.random.fold_in(key, 13), (NPART,), 0, CLASSES * ORIENT)
    strength = jax.random.uniform(jax.random.fold_in(key, 14), (NPART,), jnp.float32, 0.0, 5.0)
    aligned = jnp.take(flat_refs, picked, axis=0)
    mixed = strength[:, None] * aligned + 0.7 * noise
    return jnp.clip(mixed, -5.0, 5.0).astype(jnp.bfloat16)


def draw_shifts(key, part):
    values = jax.random.randint(jax.random.fold_in(key, 15), (TRANS, 2), -SHIFT_MAX, SHIFT_MAX + 1)
    row_index = jnp.arange(TRANS, dtype=jnp.int32)[:, None]
    col_index = jnp.arange(2, dtype=jnp.int32)[None, :]
    corner = jnp.where(col_index == 0, SHIFT_MAX, -SHIFT_MAX)
    values = jnp.where(row_index == 1, corner, values)
    values = jnp.where(row_index == 0, 0, values)
    return values.astype(jnp.int32)


def plant(result, stream_key, least, high):
    extent = result.shape
    index_at = [jax.random.randint(jax.random.fold_in(stream_key, axis), (), 0, extent[axis]) for axis in range(len(extent))]
    result = result.at[tuple(index_at)].set(least)
    longest = extent.index(max(extent))
    index_at[longest] = (index_at[longest] + 1) % extent[longest]
    return result.at[tuple(index_at)].set(high)


def setup_inputs(seed: int = 0) -> dict:
    seeds = jax.random.split(jax.random.key(seed), 7)
    return {
        "particles": draw_particles(jax.random.fold_in(seeds[6], 71), 0),
        "references": draw_references(jax.random.fold_in(seeds[6], 71), 0),
        "inv_noise": jnp.clip(jnp.exp(jax.random.uniform(seeds[2], (PIX,), jnp.float32, math.log(0.3), math.log(3.0))), 0.3, 3.0),
        "shifts": draw_shifts(jax.random.fold_in(seeds[6], 71), 0),
        "prior_class": plant(jax.random.randint(seeds[4], (NPART,), 0, CLASSES), jax.random.fold_in(seeds[4], 1), 0, CLASSES - 1).astype(jnp.int32),
        "prior_orient": plant(jax.random.randint(seeds[5], (NPART,), 0, ORIENT), jax.random.fold_in(seeds[5], 1), 0, ORIENT - 1).astype(jnp.int32),
    }


PRIOR_LOG_BOOST = 12.0


def phase_table(shifts):
    half_width = L // 2 + 1
    row_index = jnp.arange(L, dtype=jnp.int32)
    freq_y = jnp.where(row_index < L // 2, row_index, row_index - L)
    freq_y = jnp.repeat(freq_y, half_width)
    freq_x = jnp.tile(jnp.arange(half_width, dtype=jnp.int32), L)
    phase_turns = (freq_x[:, None] * shifts[None, :, 0] + freq_y[:, None] * shifts[None, :, 1]) % L
    shift_phase_radians = phase_turns.astype(jnp.float32) * (2.0 * math.pi / L)
    return jnp.concatenate([jnp.cos(shift_phase_radians), jnp.sin(shift_phase_radians)], 0).astype(jnp.bfloat16)


def correlate(reference_block, parts_real, parts_imag, inv_noise, table):
    width = parts_real.shape[1]
    ref_real = reference_block[:, :width].astype(jnp.float32)
    ref_imag = reference_block[:, width:].astype(jnp.float32)
    prod_real = inv_noise * (parts_real[:, None, :] * ref_real[None] + parts_imag[:, None, :] * ref_imag[None])
    prod_imag = inv_noise * (parts_imag[:, None, :] * ref_real[None] - parts_real[:, None, :] * ref_imag[None])
    products = jnp.concatenate([prod_real, prod_imag], -1).astype(jnp.bfloat16)
    row_count = parts_real.shape[0]
    orient_count = reference_block.shape[0]
    score_grid = jnp.dot(products.reshape(row_count * orient_count, 2 * width), table, preferred_element_type=jnp.float32)
    score_grid = score_grid.reshape(row_count, orient_count, table.shape[1])
    power = 0.5 * jnp.sum(inv_noise * (ref_real * ref_real + ref_imag * ref_imag), -1)
    return score_grid - power[None, :, None]


def project_back(posterior_floor, parts_real, parts_imag, table):
    width = parts_real.shape[1]
    row_count, orient_count, trans_count = posterior_floor.shape
    coeff = jnp.dot(posterior_floor.reshape(row_count * orient_count, trans_count), table.T, preferred_element_type=jnp.float32)
    coeff = coeff.reshape(row_count, orient_count, 2 * width)
    cos_sum = coeff[:, :, :width]
    sin_sum = coeff[:, :, width:]
    real_part = jnp.sum(parts_real[:, None, :] * cos_sum + parts_imag[:, None, :] * sin_sum, 0)
    imag_part = jnp.sum(parts_imag[:, None, :] * cos_sum - parts_real[:, None, :] * sin_sum, 0)
    return jnp.concatenate([real_part, imag_part], -1)


def reference(particles, references, inv_noise, shifts, prior_class, prior_orient):
    table = phase_table(shifts)
    parts_real = particles[:, :PIX].astype(jnp.float32)
    parts_imag = particles[:, PIX:].astype(jnp.float32)
    orient_index = jnp.arange(ORI_DEV, dtype=jnp.int32)

    def score_block(index):
        class_id = (index // N_CLS).astype(jnp.int32)
        block_id = (index % N_CLS).astype(jnp.int32)
        start = (block_id * ORI_DEV).astype(jnp.int32)
        reference_block = lax.dynamic_slice(references, (class_id, start, jnp.int32(0)), (1, ORI_DEV, FEAT))[0]
        score_grid = correlate(reference_block, parts_real, parts_imag, inv_noise, table)
        best_match = (prior_class[:, None] == class_id) & (prior_orient[:, None] == start + orient_index[None, :])
        return score_grid + jnp.where(best_match, PRIOR_LOG_BOOST, 0.0).astype(jnp.float32)[:, :, None]

    index_list = jnp.arange(CLASSES * N_CLS, dtype=jnp.int32)
    all_scores = lax.map(score_block, index_list)
    top = jnp.max(all_scores, axis=(0, 2, 3))
    total = jnp.sum(jnp.exp(all_scores - top[None, :, None, None]), axis=(0, 2, 3))
    log_norm = top + jnp.log(total)

    def back_block(index):
        posterior = jnp.exp(all_scores[index] - log_norm[:, None, None])
        weight = jnp.sum(posterior, axis=(0, 2))
        sums = project_back(posterior.astype(jnp.bfloat16), parts_real, parts_imag, table)
        return sums, weight

    sums, weights = lax.map(back_block, index_list)
    back_projection = sums.reshape(CLASSES, ORIENT, FEAT)
    class_weights = weights.reshape(CLASSES, ORIENT)
    return back_projection, class_weights, log_norm
```

```python
import functools
import math

import jax
import jax.numpy as jnp
import numpy as np
from jax import lax
from jax.experimental import pallas as pl
from jax.experimental.pallas import tpu as pltpu
from jax.sharding import PartitionSpec as P

L = 128
LANES = 128
PRIOR_LOG_BOOST = 12.0
MESH = pl.DeviceIdType.MESH
F32 = jnp.float32
BF16 = jnp.bfloat16


class Sizes:
    def __init__(self, n_dom, n_cls, parts, orient, feat, orient_all):
        self.chips = n_dom // 2
        self.n_cls = n_cls
        self.parts = parts
        self.orient = orient
        self.orient_all = orient_all
        self.feat = feat
        self.tiles = feat // 2 // LANES
        self.chunks = 5
        self.per_chunk = self.tiles // self.chunks
        self.half_rows = self.per_chunk + 1
        self.row_stride = 2 * self.half_rows
        self.block = orient * self.row_stride
        self.refs = self.chips * orient
        self.imgs = 2 * parts
        self.rows = self.imgs * self.refs
        self.group = 2 * n_cls


def kernel(
    z,
    x_hbm,
    ref_ref,
    w_ref,
    shift_ref,
    pc_ref,
    po_ref,
    cos_ref,
    sin_ref,
    bp_ref,
    cw_ref,
    ln_ref,
    xb,
    x32,
    tab,
    prior,
    ref_rows,
    ref_send,
    ref_recv,
    ref_f32,
    acc,
    power,
    top,
    total,
    stats,
    scale,
    post,
    weight,
    back_rows,
    back_send,
    back_recv,
    back_own,
    back_sum,
    x_sem,
    pair_send,
    pair_recv,
    ref_ssem,
    ref_rsem,
    stat_ssem,
    stat_rsem,
    back_ssem,
    back_rsem,
):
    dom = lax.axis_index("dom")
    cls = lax.axis_index("cls")
    chip = dom // 2
    core = lax.rem(dom, 2)
    slot = cls * 2 + core
    other = 1 - core

    def same_core(step):
        peer_chip = lax.rem(chip + step, z.chips)
        return peer_chip, (peer_chip * 2 + core, cls)

    def same_images(step):
        peer = lax.rem(slot + step, z.group)
        return peer, (chip * 2 + lax.rem(peer, 2), peer // 2)

    barrier = pltpu.get_barrier_semaphore()

    def greet_refs(step, c):
        _, device = same_core(step)
        pl.semaphore_signal(barrier, inc=1, device_id=device, device_id_type=MESH)
        return c

    def greet_stats(step, c):
        _, device = same_images(step)
        pl.semaphore_signal(barrier, inc=1, device_id=device, device_id_type=MESH)
        return c

    lax.fori_loop(1, z.chips, greet_refs, 0)
    lax.fori_loop(1, z.group, greet_stats, 0)

    own_x = pltpu.make_async_copy(x_hbm, xb.at[core], x_sem)
    own_x.start()

    for tile in range(2 * z.tiles):
        part, kt = divmod(tile, z.tiles)
        s, k = divmod(kt, z.per_chunk)
        start = s * z.block + part * z.half_rows + k
        ref_rows[pl.ds(start, z.orient, stride=z.row_stride), :] = ref_ref[
            0, :, tile * LANES : (tile + 1) * LANES
        ].astype(F32)
    for s in range(z.chunks):
        rows = ref_rows[s * z.block : (s + 1) * z.block, :].astype(BF16)
        ref_send[s] = rows
        ref_recv[chip, s] = rows
    for i in range(z.parts):
        value = (pc_ref[i] * z.orient_all + po_ref[i]).astype(F32)
        prior[core, i : i + 1, :] = jnp.full((1, LANES), value, F32)

    pl.semaphore_wait(barrier, z.chips - 1 + z.group - 1)

    def pair_copies():
        device = (chip * 2 + other, cls)
        return (
            pltpu.make_async_remote_copy(
                src_ref=x_hbm,
                dst_ref=xb.at[core],
                send_sem=pair_send.at[0],
                recv_sem=pair_recv.at[0],
                device_id=device,
                device_id_type=MESH,
            ),
            pltpu.make_async_remote_copy(
                src_ref=prior.at[core],
                dst_ref=prior.at[core],
                send_sem=pair_send.at[1],
                recv_sem=pair_recv.at[1],
                device_id=device,
                device_id_type=MESH,
            ),
        )

    pair = pair_copies()
    for copy in pair:
        copy.start()

    def ref_copy(s, step):
        peer, device = same_core(step)
        return peer, pltpu.make_async_remote_copy(
            src_ref=ref_send.at[s],
            dst_ref=ref_recv.at[chip, s],
            send_sem=ref_ssem.at[step, s],
            recv_sem=ref_rsem.at[chip, s],
            device_id=device,
            device_id_type=MESH,
        )

    def ref_arrival(s, step):
        peer, device = same_core(step)
        return pltpu.make_async_remote_copy(
            src_ref=ref_send.at[s],
            dst_ref=ref_recv.at[peer, s],
            send_sem=ref_ssem.at[step, s],
            recv_sem=ref_rsem.at[peer, s],
            device_id=device,
            device_id_type=MESH,
        )

    def send_refs(s, c):
        def to_peer(step, c):
            ref_copy(s, step)[1].start()
            return c

        return lax.fori_loop(1, z.chips, to_peer, c)

    lax.fori_loop(0, z.chunks, send_refs, 0)

    shift_x = jnp.broadcast_to(shift_ref[:, 0:1].astype(F32), (LANES, LANES))
    shift_y = jnp.broadcast_to(shift_ref[:, 1:2].astype(F32), (LANES, LANES))
    lane = lax.broadcasted_iota(jnp.int32, (1, LANES), 1)
    half_width = L // 2 + 1

    def make_table(kt, c):
        k = kt * LANES + lane
        row = (k * 4033) >> 18
        col = k - row * half_width
        row = row.astype(F32)
        col = col.astype(F32)
        for t in range(0, LANES, 8):
            turn = (col * shift_x[t : t + 8] + row * shift_y[t : t + 8]).astype(jnp.int32) & (L - 1)
            cosine = jnp.take_along_axis(
                jnp.broadcast_to(cos_ref[...], (8, LANES)), turn, axis=1, mode="promise_in_bounds"
            )
            sine = jnp.take_along_axis(
                jnp.broadcast_to(sin_ref[...], (8, LANES)), turn, axis=1, mode="promise_in_bounds"
            )
            tab[kt, t : t + 8, :LANES] = cosine.astype(BF16)
            tab[kt, t : t + 8, LANES:] = sine.astype(BF16)
        return c

    lax.fori_loop(0, z.tiles, make_table, 0)

    own_x.wait()
    for copy in pair:
        copy.wait_recv()

    def widen(tile, c):
        at = pl.multiple_of(tile * LANES, LANES)
        to = pl.multiple_of(tile * z.imgs, 8)
        for half in range(2):
            x32[pl.ds(to + half * z.parts, z.parts), :] = xb[half, :, pl.ds(at, LANES)].astype(F32)
        return c

    lax.fori_loop(0, 2 * z.tiles, widen, 0)

    def image_row(tile, i):
        return x32[pl.ds(tile * z.imgs + i, 8, stride=0), :]

    halves = z.refs // 8
    acc[...] = jnp.zeros_like(acc)
    power[...] = jnp.zeros_like(power)

    def score_chunk(s, c):
        def arrive(step, c):
            ref_arrival(s, step).wait_recv()
            return c

        lax.fori_loop(1, z.chips, arrive, 0)
        for peer in range(z.chips):
            ref_f32[peer * z.block : (peer + 1) * z.block, :] = ref_recv[peer, s].astype(F32)

        def tile_step(k, c):
            kt = s * z.per_chunk + k
            noise = w_ref[pl.ds(kt, 8, stride=0), :]
            real, imag = [], []
            for h in range(halves):
                first = h * 8 * z.row_stride + k
                a_real = ref_f32[pl.ds(first, 8, stride=z.row_stride), :]
                a_imag = ref_f32[pl.ds(first + z.half_rows, 8, stride=z.row_stride), :]
                w_real = noise * a_real
                w_imag = noise * a_imag
                power[h * 8 : (h + 1) * 8, :] += w_real * a_real + w_imag * a_imag
                real.append(w_real)
                imag.append(w_imag)
            lhs = []
            for i in range(z.imgs):
                x_real = image_row(kt, i)
                x_imag = image_row(z.tiles + kt, i)
                p_real = jnp.concatenate(
                    [real[h] * x_real + imag[h] * x_imag for h in range(halves)], 0
                )
                p_imag = jnp.concatenate(
                    [real[h] * x_imag - imag[h] * x_real for h in range(halves)], 0
                )
                lhs.append(jnp.concatenate([p_real.astype(BF16), p_imag.astype(BF16)], 1))
            acc[...] += lax.dot_general(
                jnp.concatenate(lhs, 0),
                tab[kt],
                (((1,), (1,)), ((), ())),
                preferred_element_type=F32,
            )
            return c

        return lax.fori_loop(0, z.per_chunk, tile_step, c)

    lax.fori_loop(0, z.chunks, score_chunk, 0)

    row = lax.broadcasted_iota(jnp.int32, (z.refs, LANES), 0)
    class_id = 2 * (row // z.orient) + core
    ref_id = class_id * z.orient_all + cls * z.orient + lax.rem(row, z.orient)
    ref_id = ref_id.astype(F32)
    half_power = 0.5 * jnp.sum(power[...], axis=1, keepdims=True)
    for i in range(z.imgs):
        half, il = divmod(i, z.parts)
        block = acc[i * z.refs : (i + 1) * z.refs, :] - half_power
        block = block + jnp.where(prior[half, il : il + 1, :] == ref_id, PRIOR_LOG_BOOST, 0.0)
        acc[i * z.refs : (i + 1) * z.refs, :] = block
        top[i : i + 1, :] = jnp.max(block, axis=0, keepdims=True)
    top[...] = jnp.broadcast_to(jnp.max(top[...], axis=1, keepdims=True), top.shape)
    for i in range(z.imgs):
        block = jnp.exp(acc[i * z.refs : (i + 1) * z.refs, :] - top[i : i + 1, :])
        acc[i * z.refs : (i + 1) * z.refs, :] = block
        total[i : i + 1, :] = jnp.sum(block, axis=0, keepdims=True)
    sums = jnp.sum(total[...], axis=1, keepdims=True)
    lane8 = lax.broadcasted_iota(jnp.int32, (8, LANES), 1)
    groups = z.imgs // 8
    packed = jnp.zeros((8, LANES), F32)
    for v in range(groups):
        packed = jnp.where(lane8 == v, top[v * 8 : (v + 1) * 8, :], packed)
        packed = jnp.where(lane8 == groups + v, sums[v * 8 : (v + 1) * 8, :], packed)
    stats[slot] = packed

    def stat_copy(step):
        _, device = same_images(step)
        return pltpu.make_async_remote_copy(
            src_ref=stats.at[slot],
            dst_ref=stats.at[slot],
            send_sem=stat_ssem.at[step],
            recv_sem=stat_rsem.at[slot],
            device_id=device,
            device_id_type=MESH,
        )

    def stat_arrival(step):
        peer, device = same_images(step)
        return pltpu.make_async_remote_copy(
            src_ref=stats.at[peer],
            dst_ref=stats.at[peer],
            send_sem=stat_ssem.at[step],
            recv_sem=stat_rsem.at[peer],
            device_id=device,
            device_id_type=MESH,
        )

    def send_stat(step, c):
        stat_copy(step).start()
        return c

    def take_stat(step, c):
        stat_arrival(step).wait_recv()
        return c

    lax.fori_loop(1, z.group, send_stat, 0)
    lax.fori_loop(1, z.group, take_stat, 0)

    all_top = stats[0]
    for g in range(1, z.group):
        all_top = jnp.maximum(all_top, stats[g])
    all_total = jnp.zeros((8, LANES), F32)
    for g in range(z.group):
        part = stats[g]
        all_total = all_total + jnp.exp(part - all_top) * pltpu.roll(part, LANES - groups, 1)
    log_norm = all_top + jnp.log(all_total)
    rescale = jnp.exp(packed - log_norm)
    for v in range(groups):
        scale[v * 8 : (v + 1) * 8, :] = jnp.broadcast_to(rescale[:, v : v + 1], (8, LANES))
        total[v * 8 : (v + 1) * 8, :] = jnp.broadcast_to(log_norm[:, v : v + 1], (8, LANES))
    mine = total[pl.ds(pl.multiple_of(core * z.parts, 8), z.parts), :]
    diagonal = lax.broadcasted_iota(jnp.int32, (z.parts, LANES), 0) == lax.broadcasted_iota(
        jnp.int32, (z.parts, LANES), 1
    )
    ln_ref[...] = jnp.sum(jnp.where(diagonal, mine, 0.0), axis=0, keepdims=True)[:, : z.parts]

    mass = jnp.zeros((z.refs, LANES), F32)
    for i in range(z.imgs):
        block = acc[i * z.refs : (i + 1) * z.refs, :] * scale[i : i + 1, :]
        mass = mass + block
        post[i * z.refs : (i + 1) * z.refs, :] = block.astype(BF16)
    weight[...] = jnp.broadcast_to(jnp.sum(mass, axis=1, keepdims=True), weight.shape)

    def back_copy(s, step):
        peer, device = same_core(step)
        return pltpu.make_async_remote_copy(
            src_ref=back_send.at[peer, s],
            dst_ref=back_recv.at[chip, s],
            send_sem=back_ssem.at[step, s],
            recv_sem=back_rsem.at[chip, s],
            device_id=device,
            device_id_type=MESH,
        )

    def back_arrival(s, step):
        peer, device = same_core(step)
        return pltpu.make_async_remote_copy(
            src_ref=back_send.at[peer, s],
            dst_ref=back_recv.at[peer, s],
            send_sem=back_ssem.at[step, s],
            recv_sem=back_rsem.at[peer, s],
            device_id=device,
            device_id_type=MESH,
        )

    def back_chunk(s, c):
        def tile_step(k, c):
            kt = s * z.per_chunk + k
            coeff = jnp.dot(post[...], tab[kt], preferred_element_type=F32)
            real = [jnp.zeros((8, LANES), F32) for _ in range(halves)]
            imag = [jnp.zeros((8, LANES), F32) for _ in range(halves)]
            for i in range(z.imgs):
                x_real = image_row(kt, i)
                x_imag = image_row(z.tiles + kt, i)
                for h in range(halves):
                    at = i * z.refs + h * 8
                    cosine = coeff[at : at + 8, :LANES]
                    sine = coeff[at : at + 8, LANES:]
                    real[h] = real[h] + (x_real * cosine + x_imag * sine)
                    imag[h] = imag[h] + (x_imag * cosine - x_real * sine)
            for h in range(halves):
                first = h * 8 * z.row_stride + k
                back_rows[pl.ds(first, 8, stride=z.row_stride), :] = real[h]
                back_rows[pl.ds(first + z.half_rows, 8, stride=z.row_stride), :] = imag[h]
            return c

        lax.fori_loop(0, z.per_chunk, tile_step, 0)
        high = weight[...].astype(BF16).astype(F32)
        low = weight[...] - high
        for h in range(halves):
            first = h * 8 * z.row_stride + z.per_chunk
            rows = slice(h * 8, (h + 1) * 8)
            back_rows[pl.ds(first, 8, stride=z.row_stride), :] = high[rows]
            back_rows[pl.ds(first + z.half_rows, 8, stride=z.row_stride), :] = low[rows]
        for peer in range(z.chips):
            back_send[peer, s] = back_rows[peer * z.block : (peer + 1) * z.block, :].astype(BF16)
        back_own[s] = back_rows[pl.ds(pl.multiple_of(chip * z.block, 8), z.block), :]

        def to_peer(step, c):
            back_copy(s, step).start()
            return c

        return lax.fori_loop(1, z.chips, to_peer, c)

    lax.fori_loop(0, z.chunks, back_chunk, 0)

    def gather_chunk(s, c):
        def arrive(step, c):
            back_arrival(s, step).wait_recv()
            return c

        lax.fori_loop(1, z.chips, arrive, 0)

        def add(step, got):
            peer, _ = same_core(step)
            return got + back_recv[peer, s].astype(F32)

        back_sum[pl.ds(pl.multiple_of(s * z.block, 8), z.block), :] = lax.fori_loop(
            1, z.chips, add, back_own[s]
        )
        return c

    lax.fori_loop(0, z.chunks, gather_chunk, 0)
    for tile in range(2 * z.tiles):
        part, kt = divmod(tile, z.tiles)
        s, k = divmod(kt, z.per_chunk)
        start = s * z.block + part * z.half_rows + k
        bp_ref[0, :, tile * LANES : (tile + 1) * LANES] = back_sum[
            pl.ds(start, z.orient, stride=z.row_stride), :
        ]
    line = jnp.zeros((1, LANES), F32)
    for o in range(z.orient):
        at = o * z.row_stride + z.per_chunk
        both = back_sum[at : at + 1, :] + back_sum[at + z.half_rows : at + z.half_rows + 1, :]
        line = jnp.where(lane == o, both, line)
    cw_ref[...] = line[:, : z.orient]

    for copy in pair:
        copy.wait_send()

    def drain_chunk(s, c):
        def drain(step, c):
            ref_copy(s, step)[1].wait_send()
            back_copy(s, step).wait_send()
            return c

        return lax.fori_loop(1, z.chips, drain, c)

    def drain_stat(step, c):
        stat_copy(step).wait_send()
        return c

    lax.fori_loop(0, z.chunks, drain_chunk, 0)
    lax.fori_loop(1, z.group, drain_stat, 0)


def on_device(z, particles, references, inv_noise, shifts, prior_class, prior_orient):
    angle = (np.arange(L, dtype=np.float32) * np.float32(2.0 * math.pi / L)).astype(np.float64)
    cosine = jnp.asarray(np.cos(angle).astype(np.float32)[None])
    sine = jnp.asarray(np.sin(angle).astype(np.float32)[None])
    vmem = pl.BlockSpec(memory_space=pltpu.VMEM)
    smem = pl.BlockSpec(memory_space=pltpu.SMEM)
    dma = pltpu.SemaphoreType.DMA
    blocks = (z.chips, z.chunks, z.block, LANES)
    flops = 4 * z.rows * z.feat * LANES
    bp, cw, ln = pl.pallas_call(
        functools.partial(kernel, z),
        out_shape=(
            jax.ShapeDtypeStruct((1, z.orient, z.feat), F32),
            jax.ShapeDtypeStruct((1, z.orient), F32),
            jax.ShapeDtypeStruct((1, z.parts), F32),
        ),
        in_specs=[pl.BlockSpec(memory_space=pl.ANY), vmem, vmem, vmem, smem, smem, vmem, vmem],
        out_specs=(vmem, vmem, vmem),
        scratch_shapes=[
            pltpu.VMEM((2, z.parts, z.feat), BF16),
            pltpu.VMEM((2 * z.tiles * z.imgs, LANES), F32),
            pltpu.VMEM((z.tiles, LANES, 2 * LANES), BF16),
            pltpu.VMEM((2, z.parts, LANES), F32),
            pltpu.VMEM((z.chunks * z.block, LANES), F32),
            pltpu.VMEM((z.chunks, z.block, LANES), BF16),
            pltpu.VMEM(blocks, BF16),
            pltpu.VMEM((z.chips * z.block, LANES), F32),
            pltpu.VMEM((z.rows, LANES), F32),
            pltpu.VMEM((z.refs, LANES), F32),
            pltpu.VMEM((z.imgs, LANES), F32),
            pltpu.VMEM((z.imgs, LANES), F32),
            pltpu.VMEM((z.group, 8, LANES), F32),
            pltpu.VMEM((z.imgs, LANES), F32),
            pltpu.VMEM((z.rows, LANES), BF16),
            pltpu.VMEM((z.refs, LANES), F32),
            pltpu.VMEM((z.chips * z.block, LANES), F32),
            pltpu.VMEM(blocks, BF16),
            pltpu.VMEM(blocks, BF16),
            pltpu.VMEM((z.chunks, z.block, LANES), F32),
            pltpu.VMEM((z.chunks * z.block, LANES), F32),
            dma,
            dma((2,)),
            dma((2,)),
            dma((z.chips, z.chunks)),
            dma((z.chips, z.chunks)),
            dma((z.group,)),
            dma((z.group,)),
            dma((z.chips, z.chunks)),
            dma((z.chips, z.chunks)),
        ],
        compiler_params=pltpu.CompilerParams(
            collective_id=0, has_side_effects=True, vmem_limit_bytes=40 * 2**20
        ),
        cost_estimate=pl.CostEstimate(
            flops=flops, bytes_accessed=4 * 2**20, transcendentals=z.rows * LANES
        ),
    )(
        particles,
        references,
        inv_noise.reshape(z.tiles, LANES),
        shifts,
        prior_class,
        prior_orient,
        cosine,
        sine,
    )
    return bp, cw, ln.reshape(z.parts)


def solution(mesh):
    def body(particles, references, inv_noise, shifts, prior_class, prior_orient):
        n_dom, n_cls = lax.axis_size("dom"), lax.axis_size("cls")
        z = Sizes(
            n_dom,
            n_cls,
            particles.shape[0],
            references.shape[1],
            particles.shape[1],
            references.shape[1] * n_cls,
        )
        return on_device(z, particles, references, inv_noise, shifts, prior_class, prior_orient)

    placed = (P("dom", None), P("dom", "cls", None), P(), P(), P("dom"), P("dom"))
    return jax.shard_map(
        body,
        mesh=mesh,
        in_specs=placed,
        out_specs=(P("dom", "cls", None), P("dom", "cls"), P("dom")),
        check_vma=False,
    )
```

```python
import functools
import math

import jax
import jax.numpy as jnp
import numpy as np
from jax import lax
from jax.experimental import pallas as pl
from jax.experimental.pallas import tpu as pltpu
from jax.sharding import PartitionSpec as P

L = 128
LANES = 128
PRIOR_LOG_BOOST = 12.0
MESH = pl.DeviceIdType.MESH
F32 = jnp.float32
BF16 = jnp.bfloat16


class Sizes:
    def __init__(self, n_dom, n_cls, parts, orient, feat, orient_all):
        self.chips = n_dom // 2
        self.n_cls = n_cls
        self.parts = parts
        self.orient = orient
        self.orient_all = orient_all
        self.feat = feat
        self.tiles = feat // 2 // LANES
        self.chunks = 5
        self.per_chunk = self.tiles // self.chunks
        self.half_rows = self.per_chunk + 1
        self.row_stride = 2 * self.half_rows
        self.block = orient * self.row_stride
        self.refs = self.chips * orient
        self.imgs = 2 * parts
        self.rows = self.imgs * self.refs
        self.group = 2 * n_cls


def kernel(
    z,
    x_hbm,
    ref_ref,
    w_ref,
    shift_ref,
    pc_ref,
    po_ref,
    cos_ref,
    sin_ref,
    bp_ref,
    cw_ref,
    ln_ref,
    xb,
    x32,
    tab,
    prior,
    ref_rows,
    ref_send,
    ref_recv,
    ref_f32,
    acc,
    power,
    top,
    total,
    stats,
    scale,
    post,
    weight,
    back_rows,
    back_send,
    back_recv,
    back_own,
    back_sum,
    x_sem,
    pair_send,
    pair_recv,
    ref_ssem,
    ref_rsem,
    stat_ssem,
    stat_rsem,
    back_ssem,
    back_rsem,
):
    dom = lax.axis_index("dom")
    cls = lax.axis_index("cls")
    chip = dom // 2
    core = lax.rem(dom, 2)
    slot = cls * 2 + core
    other = 1 - core

    def same_core(step):
        peer_chip = lax.rem(chip + step, z.chips)
        return peer_chip, (peer_chip * 2 + core, cls)

    def same_images(step):
        peer = lax.rem(slot + step, z.group)
        return peer, (chip * 2 + lax.rem(peer, 2), peer // 2)

    barrier = pltpu.get_barrier_semaphore()

    def greet_refs(step, c):
        _, device = same_core(step)
        pl.semaphore_signal(barrier, inc=1, device_id=device, device_id_type=MESH)
        return c

    def greet_stats(step, c):
        _, device = same_images(step)
        pl.semaphore_signal(barrier, inc=1, device_id=device, device_id_type=MESH)
        return c

    lax.fori_loop(1, z.chips, greet_refs, 0)
    lax.fori_loop(1, z.group, greet_stats, 0)

    own_x = pltpu.make_async_copy(x_hbm, xb.at[core], x_sem)
    own_x.start()

    for tile in range(2 * z.tiles):
        part, kt = divmod(tile, z.tiles)
        s, k = divmod(kt, z.per_chunk)
        start = s * z.block + part * z.half_rows + k
        ref_rows[pl.ds(start, z.orient, stride=z.row_stride), :] = ref_ref[
            0, :, tile * LANES : (tile + 1) * LANES
        ].astype(F32)
    for s in range(z.chunks):
        rows = ref_rows[s * z.block : (s + 1) * z.block, :].astype(BF16)
        ref_send[s] = rows
        ref_recv[chip, s] = rows
    for i in range(z.parts):
        value = (pc_ref[i] * z.orient_all + po_ref[i]).astype(F32)
        prior[core, i : i + 1, :] = jnp.full((1, LANES), value, F32)

    pl.semaphore_wait(barrier, z.chips - 1 + z.group - 1)

    def pair_copies():
        device = (chip * 2 + other, cls)
        return (
            pltpu.make_async_remote_copy(
                src_ref=x_hbm,
                dst_ref=xb.at[core],
                send_sem=pair_send.at[0],
                recv_sem=pair_recv.at[0],
                device_id=device,
                device_id_type=MESH,
            ),
            pltpu.make_async_remote_copy(
                src_ref=prior.at[core],
                dst_ref=prior.at[core],
                send_sem=pair_send.at[1],
                recv_sem=pair_recv.at[1],
                device_id=device,
                device_id_type=MESH,
            ),
        )

    pair = pair_copies()
    for copy in pair:
        copy.start()

    def ref_copy(s, step):
        peer, device = same_core(step)
        return peer, pltpu.make_async_remote_copy(
            src_ref=ref_send.at[s],
            dst_ref=ref_recv.at[chip, s],
            send_sem=ref_ssem.at[step, s],
            recv_sem=ref_rsem.at[chip, s],
            device_id=device,
            device_id_type=MESH,
        )

    def ref_arrival(s, step):
        peer, device = same_core(step)
        return pltpu.make_async_remote_copy(
            src_ref=ref_send.at[s],
            dst_ref=ref_recv.at[peer, s],
            send_sem=ref_ssem.at[step, s],
            recv_sem=ref_rsem.at[peer, s],
            device_id=device,
            device_id_type=MESH,
        )

    def send_refs(s, c):
        def to_peer(step, c):
            ref_copy(s, step)[1].start()
            return c

        return lax.fori_loop(1, z.chips, to_peer, c)

    lax.fori_loop(0, z.chunks, send_refs, 0)

    lane = lax.broadcasted_iota(jnp.int32, (1, LANES), 1)
    half_width = L // 2 + 1

    def look_up(turn):
        turn = turn.astype(jnp.int32) & (L - 1)
        return tuple(
            jnp.take_along_axis(
                jnp.broadcast_to(ref[...], (8, LANES)), turn, axis=1, mode="promise_in_bounds"
            )
            for ref in (cos_ref, sin_ref)
        )

    lane8 = lax.broadcasted_iota(jnp.int32, (8, LANES), 1)
    first_row = jnp.where(lane8 >= half_width, 1, 0)
    first_col = lane8 - half_width * first_row
    rows_on, rows_over = divmod(LANES, half_width)
    rows_on, rows_back = rows_on + 1, half_width - rows_over
    span = 8
    for t0 in range(0, LANES, 8 * span):
        start, turns = [], []
        for v in range(span):
            rows = slice(t0 + 8 * v, t0 + 8 * v + 8)
            shift_x = jnp.broadcast_to(shift_ref[rows, 0:1].astype(F32), (8, LANES))
            shift_y = jnp.broadcast_to(shift_ref[rows, 1:2].astype(F32), (8, LANES))
            start.append(
                look_up(first_col.astype(F32) * shift_x + first_row.astype(F32) * shift_y)
            )
            turns.append(
                (
                    look_up(rows_on * shift_y - rows_back * shift_x),
                    look_up((rows_on - 1) * shift_y + rows_over * shift_x),
                )
            )

        def make_table(step, carry):
            now, col = carry
            for j in range(z.per_chunk):
                kt = step * z.per_chunk + j
                near = col >= rows_back
                col = jnp.where(near, col - rows_back, col + rows_over)
                after = []
                for v in range(span):
                    cosine, sine = now[v]
                    rows = slice(t0 + 8 * v, t0 + 8 * v + 8)
                    tab[kt, rows, :LANES] = cosine.astype(BF16)
                    tab[kt, rows, LANES:] = sine.astype(BF16)
                    turn_cos = jnp.where(near, turns[v][0][0], turns[v][1][0])
                    turn_sin = jnp.where(near, turns[v][0][1], turns[v][1][1])
                    after.append(
                        (
                            cosine * turn_cos - sine * turn_sin,
                            sine * turn_cos + cosine * turn_sin,
                        )
                    )
                now = tuple(after)
            return now, col

        lax.fori_loop(0, z.chunks, make_table, (tuple(start), first_col))

    own_x.wait()
    for copy in pair:
        copy.wait_recv()

    def widen(tile, c):
        at = pl.multiple_of(tile * LANES, LANES)
        to = pl.multiple_of(tile * z.imgs, 8)
        for half in range(2):
            x32[pl.ds(to + half * z.parts, z.parts), :] = xb[half, :, pl.ds(at, LANES)].astype(F32)
        return c

    lax.fori_loop(0, 2 * z.tiles, widen, 0)

    def image_row(tile, i):
        return x32[pl.ds(tile * z.imgs + i, 8, stride=0), :]

    halves = z.refs // 8
    acc[...] = jnp.zeros_like(acc)
    power[...] = jnp.zeros_like(power)

    def score_chunk(s, c):
        def arrive(step, c):
            ref_arrival(s, step).wait_recv()
            return c

        lax.fori_loop(1, z.chips, arrive, 0)
        for peer in range(z.chips):
            ref_f32[peer * z.block : (peer + 1) * z.block, :] = ref_recv[peer, s].astype(F32)

        def tile_step(k):
            kt = s * z.per_chunk + k
            noise = w_ref[pl.ds(kt, 8, stride=0), :]
            real, imag = [], []
            for h in range(halves):
                first = h * 8 * z.row_stride + k
                a_real = ref_f32[pl.ds(first, 8, stride=z.row_stride), :]
                a_imag = ref_f32[pl.ds(first + z.half_rows, 8, stride=z.row_stride), :]
                w_real = noise * a_real
                w_imag = noise * a_imag
                power[h * 8 : (h + 1) * 8, :] += w_real * a_real + w_imag * a_imag
                real.append(w_real)
                imag.append(w_imag)
            lhs = []
            for i in range(z.imgs):
                x_real = image_row(kt, i)
                x_imag = image_row(z.tiles + kt, i)
                p_real = jnp.concatenate(
                    [real[h] * x_real + imag[h] * x_imag for h in range(halves)], 0
                )
                p_imag = jnp.concatenate(
                    [real[h] * x_imag - imag[h] * x_real for h in range(halves)], 0
                )
                lhs.append(jnp.concatenate([p_real.astype(BF16), p_imag.astype(BF16)], 1))
            acc[...] += lax.dot_general(
                jnp.concatenate(lhs, 0),
                tab[kt],
                (((1,), (1,)), ((), ())),
                preferred_element_type=F32,
            )

        for k in range(z.per_chunk):
            tile_step(k)
        return c

    lax.fori_loop(0, z.chunks, score_chunk, 0)

    row = lax.broadcasted_iota(jnp.int32, (z.refs, LANES), 0)
    class_id = 2 * (row // z.orient) + core
    ref_id = class_id * z.orient_all + cls * z.orient + lax.rem(row, z.orient)
    ref_id = ref_id.astype(F32)
    half_power = 0.5 * jnp.sum(power[...], axis=1, keepdims=True)
    for i in range(z.imgs):
        half, il = divmod(i, z.parts)
        block = acc[i * z.refs : (i + 1) * z.refs, :] - half_power
        block = block + jnp.where(prior[half, il : il + 1, :] == ref_id, PRIOR_LOG_BOOST, 0.0)
        acc[i * z.refs : (i + 1) * z.refs, :] = block
        top[i : i + 1, :] = jnp.max(block, axis=0, keepdims=True)
    top[...] = jnp.broadcast_to(jnp.max(top[...], axis=1, keepdims=True), top.shape)
    for i in range(z.imgs):
        block = jnp.exp(acc[i * z.refs : (i + 1) * z.refs, :] - top[i : i + 1, :])
        acc[i * z.refs : (i + 1) * z.refs, :] = block
        total[i : i + 1, :] = jnp.sum(block, axis=0, keepdims=True)
    sums = jnp.sum(total[...], axis=1, keepdims=True)
    groups = z.imgs // 8
    packed = jnp.zeros((8, LANES), F32)
    for v in range(groups):
        packed = jnp.where(lane8 == v, top[v * 8 : (v + 1) * 8, :], packed)
        packed = jnp.where(lane8 == groups + v, sums[v * 8 : (v + 1) * 8, :], packed)
    stats[slot] = packed

    def stat_copy(step):
        _, device = same_images(step)
        return pltpu.make_async_remote_copy(
            src_ref=stats.at[slot],
            dst_ref=stats.at[slot],
            send_sem=stat_ssem.at[step],
            recv_sem=stat_rsem.at[slot],
            device_id=device,
            device_id_type=MESH,
        )

    def stat_arrival(step):
        peer, device = same_images(step)
        return pltpu.make_async_remote_copy(
            src_ref=stats.at[peer],
            dst_ref=stats.at[peer],
            send_sem=stat_ssem.at[step],
            recv_sem=stat_rsem.at[peer],
            device_id=device,
            device_id_type=MESH,
        )

    def send_stat(step, c):
        stat_copy(step).start()
        return c

    def take_stat(step, c):
        stat_arrival(step).wait_recv()
        return c

    lax.fori_loop(1, z.group, send_stat, 0)
    lax.fori_loop(1, z.group, take_stat, 0)

    all_top = stats[0]
    for g in range(1, z.group):
        all_top = jnp.maximum(all_top, stats[g])
    all_total = jnp.zeros((8, LANES), F32)
    for g in range(z.group):
        part = stats[g]
        all_total = all_total + jnp.exp(part - all_top) * pltpu.roll(part, LANES - groups, 1)
    log_norm = all_top + jnp.log(all_total)
    rescale = jnp.exp(packed - log_norm)
    for v in range(groups):
        scale[v * 8 : (v + 1) * 8, :] = jnp.broadcast_to(rescale[:, v : v + 1], (8, LANES))
        total[v * 8 : (v + 1) * 8, :] = jnp.broadcast_to(log_norm[:, v : v + 1], (8, LANES))
    mine = total[pl.ds(pl.multiple_of(core * z.parts, 8), z.parts), :]
    diagonal = lax.broadcasted_iota(jnp.int32, (z.parts, LANES), 0) == lax.broadcasted_iota(
        jnp.int32, (z.parts, LANES), 1
    )
    ln_ref[...] = jnp.sum(jnp.where(diagonal, mine, 0.0), axis=0, keepdims=True)[:, : z.parts]

    mass = jnp.zeros((z.refs, LANES), F32)
    for i in range(z.imgs):
        block = acc[i * z.refs : (i + 1) * z.refs, :] * scale[i : i + 1, :]
        mass = mass + block
        post[i * z.refs : (i + 1) * z.refs, :] = block.astype(BF16)
    weight[...] = jnp.broadcast_to(jnp.sum(mass, axis=1, keepdims=True), weight.shape)

    def back_copy(s, step):
        peer, device = same_core(step)
        return pltpu.make_async_remote_copy(
            src_ref=back_send.at[peer, s],
            dst_ref=back_recv.at[chip, s],
            send_sem=back_ssem.at[step, s],
            recv_sem=back_rsem.at[chip, s],
            device_id=device,
            device_id_type=MESH,
        )

    def back_arrival(s, step):
        peer, device = same_core(step)
        return pltpu.make_async_remote_copy(
            src_ref=back_send.at[peer, s],
            dst_ref=back_recv.at[peer, s],
            send_sem=back_ssem.at[step, s],
            recv_sem=back_rsem.at[peer, s],
            device_id=device,
            device_id_type=MESH,
        )

    def back_chunk(s, c):
        def tile_step(k):
            kt = s * z.per_chunk + k
            coeff = jnp.dot(post[...], tab[kt], preferred_element_type=F32)
            real = [jnp.zeros((8, LANES), F32) for _ in range(halves)]
            imag = [jnp.zeros((8, LANES), F32) for _ in range(halves)]
            for i in range(z.imgs):
                x_real = image_row(kt, i)
                x_imag = image_row(z.tiles + kt, i)
                for h in range(halves):
                    at = i * z.refs + h * 8
                    cosine = coeff[at : at + 8, :LANES]
                    sine = coeff[at : at + 8, LANES:]
                    real[h] = real[h] + (x_real * cosine + x_imag * sine)
                    imag[h] = imag[h] + (x_imag * cosine - x_real * sine)
            for h in range(halves):
                first = h * 8 * z.row_stride + k
                back_rows[pl.ds(first, 8, stride=z.row_stride), :] = real[h]
                back_rows[pl.ds(first + z.half_rows, 8, stride=z.row_stride), :] = imag[h]

        for k in range(z.per_chunk):
            tile_step(k)
        high = weight[...].astype(BF16).astype(F32)
        low = weight[...] - high
        for h in range(halves):
            first = h * 8 * z.row_stride + z.per_chunk
            rows = slice(h * 8, (h + 1) * 8)
            back_rows[pl.ds(first, 8, stride=z.row_stride), :] = high[rows]
            back_rows[pl.ds(first + z.half_rows, 8, stride=z.row_stride), :] = low[rows]
        for peer in range(z.chips):
            back_send[peer, s] = back_rows[peer * z.block : (peer + 1) * z.block, :].astype(BF16)
        back_own[s] = back_rows[pl.ds(pl.multiple_of(chip * z.block, 8), z.block), :]

        def to_peer(step, c):
            back_copy(s, step).start()
            return c

        return lax.fori_loop(1, z.chips, to_peer, c)

    lax.fori_loop(0, z.chunks, back_chunk, 0)

    def gather_chunk(s, c):
        def arrive(step, c):
            back_arrival(s, step).wait_recv()
            return c

        lax.fori_loop(1, z.chips, arrive, 0)

        def add(step, got):
            peer, _ = same_core(step)
            return got + back_recv[peer, s].astype(F32)

        back_sum[pl.ds(pl.multiple_of(s * z.block, 8), z.block), :] = lax.fori_loop(
            1, z.chips, add, back_own[s]
        )
        return c

    lax.fori_loop(0, z.chunks, gather_chunk, 0)
    for tile in range(2 * z.tiles):
        part, kt = divmod(tile, z.tiles)
        s, k = divmod(kt, z.per_chunk)
        start = s * z.block + part * z.half_rows + k
        bp_ref[0, :, tile * LANES : (tile + 1) * LANES] = back_sum[
            pl.ds(start, z.orient, stride=z.row_stride), :
        ]
    line = jnp.zeros((1, LANES), F32)
    for o in range(z.orient):
        at = o * z.row_stride + z.per_chunk
        both = back_sum[at : at + 1, :] + back_sum[at + z.half_rows : at + z.half_rows + 1, :]
        line = jnp.where(lane == o, both, line)
    cw_ref[...] = line[:, : z.orient]

    for copy in pair:
        copy.wait_send()

    def drain_chunk(s, c):
        def drain(step, c):
            ref_copy(s, step)[1].wait_send()
            back_copy(s, step).wait_send()
            return c

        return lax.fori_loop(1, z.chips, drain, c)

    def drain_stat(step, c):
        stat_copy(step).wait_send()
        return c

    lax.fori_loop(0, z.chunks, drain_chunk, 0)
    lax.fori_loop(1, z.group, drain_stat, 0)


def on_device(z, particles, references, inv_noise, shifts, prior_class, prior_orient):
    angle = (np.arange(L, dtype=np.float32) * np.float32(2.0 * math.pi / L)).astype(np.float64)
    cosine = jnp.asarray(np.cos(angle).astype(np.float32)[None])
    sine = jnp.asarray(np.sin(angle).astype(np.float32)[None])
    vmem = pl.BlockSpec(memory_space=pltpu.VMEM)
    smem = pl.BlockSpec(memory_space=pltpu.SMEM)
    dma = pltpu.SemaphoreType.DMA
    blocks = (z.chips, z.chunks, z.block, LANES)
    flops = 4 * z.rows * z.feat * LANES
    bp, cw, ln = pl.pallas_call(
        functools.partial(kernel, z),
        out_shape=(
            jax.ShapeDtypeStruct((1, z.orient, z.feat), F32),
            jax.ShapeDtypeStruct((1, z.orient), F32),
            jax.ShapeDtypeStruct((1, z.parts), F32),
        ),
        in_specs=[pl.BlockSpec(memory_space=pl.ANY), vmem, vmem, vmem, smem, smem, vmem, vmem],
        out_specs=(vmem, vmem, vmem),
        scratch_shapes=[
            pltpu.VMEM((2, z.parts, z.feat), BF16),
            pltpu.VMEM((2 * z.tiles * z.imgs, LANES), F32),
            pltpu.VMEM((z.tiles, LANES, 2 * LANES), BF16),
            pltpu.VMEM((2, z.parts, LANES), F32),
            pltpu.VMEM((z.chunks * z.block, LANES), F32),
            pltpu.VMEM((z.chunks, z.block, LANES), BF16),
            pltpu.VMEM(blocks, BF16),
            pltpu.VMEM((z.chips * z.block, LANES), F32),
            pltpu.VMEM((z.rows, LANES), F32),
            pltpu.VMEM((z.refs, LANES), F32),
            pltpu.VMEM((z.imgs, LANES), F32),
            pltpu.VMEM((z.imgs, LANES), F32),
            pltpu.VMEM((z.group, 8, LANES), F32),
            pltpu.VMEM((z.imgs, LANES), F32),
            pltpu.VMEM((z.rows, LANES), BF16),
            pltpu.VMEM((z.refs, LANES), F32),
            pltpu.VMEM((z.chips * z.block, LANES), F32),
            pltpu.VMEM(blocks, BF16),
            pltpu.VMEM(blocks, BF16),
            pltpu.VMEM((z.chunks, z.block, LANES), F32),
            pltpu.VMEM((z.chunks * z.block, LANES), F32),
            dma,
            dma((2,)),
            dma((2,)),
            dma((z.chips, z.chunks)),
            dma((z.chips, z.chunks)),
            dma((z.group,)),
            dma((z.group,)),
            dma((z.chips, z.chunks)),
            dma((z.chips, z.chunks)),
        ],
        compiler_params=pltpu.CompilerParams(
            collective_id=0, has_side_effects=True, vmem_limit_bytes=40 * 2**20
        ),
        cost_estimate=pl.CostEstimate(
            flops=flops, bytes_accessed=4 * 2**20, transcendentals=z.rows * LANES
        ),
    )(
        particles,
        references,
        inv_noise.reshape(z.tiles, LANES),
        shifts,
        prior_class,
        prior_orient,
        cosine,
        sine,
    )
    return bp, cw, ln.reshape(z.parts)


def solution(mesh):
    def body(particles, references, inv_noise, shifts, prior_class, prior_orient):
        n_dom, n_cls = lax.axis_size("dom"), lax.axis_size("cls")
        z = Sizes(
            n_dom,
            n_cls,
            particles.shape[0],
            references.shape[1],
            particles.shape[1],
            references.shape[1] * n_cls,
        )
        return on_device(z, particles, references, inv_noise, shifts, prior_class, prior_orient)

    placed = (P("dom", None), P("dom", "cls", None), P(), P(), P("dom"), P("dom"))
    return jax.shard_map(
        body,
        mesh=mesh,
        in_specs=placed,
        out_specs=(P("dom", "cls", None), P("dom", "cls"), P("dom")),
        check_vma=False,
    )
```

```python
import functools
import math

import jax
import jax.numpy as jnp
import numpy as np
from jax import lax
from jax.experimental import pallas as pl
from jax.experimental.pallas import tpu as pltpu
from jax.sharding import PartitionSpec as P

L = 128
LANES = 128
PRIOR_LOG_BOOST = 12.0
MESH = pl.DeviceIdType.MESH
F32 = jnp.float32
BF16 = jnp.bfloat16


class Sizes:
    def __init__(self, n_dom, n_cls, parts, orient, feat, orient_all):
        self.chips = n_dom // 2
        self.n_cls = n_cls
        self.parts = parts
        self.orient = orient
        self.orient_all = orient_all
        self.feat = feat
        self.tiles = feat // 2 // LANES
        self.chunks = 5
        self.per_chunk = self.tiles // self.chunks
        self.half_rows = self.per_chunk + 1
        self.row_stride = 2 * self.half_rows
        self.block = orient * self.row_stride
        self.refs = self.chips * orient
        self.imgs = 2 * parts
        self.rows = self.imgs * self.refs
        self.group = 2 * n_cls


def kernel(
    z,
    x_hbm,
    ref_hbm,
    w_hbm,
    shift_hbm,
    pc_hbm,
    po_hbm,
    circle_hbm,
    sum_ref,
    ln_ref,
    ref_ref,
    w_ref,
    shift_ref,
    pc_ref,
    po_ref,
    circle_ref,
    xb,
    x32,
    tab,
    prior,
    ref_rows,
    ref_send,
    ref_recv,
    ref_f32,
    acc,
    power,
    top,
    total,
    stats,
    scale,
    post,
    weight,
    back_rows,
    back_send,
    back_recv,
    back_own,
    x_sem,
    in_sem,
    pair_send,
    pair_recv,
    ref_ssem,
    ref_rsem,
    stat_ssem,
    stat_rsem,
    back_ssem,
    back_rsem,
):
    dom = lax.axis_index("dom")
    cls = lax.axis_index("cls")
    chip = dom // 2
    core = lax.rem(dom, 2)
    slot = cls * 2 + core
    other = 1 - core

    own_x = pltpu.make_async_copy(x_hbm, xb.at[core], x_sem)
    small = [
        pltpu.make_async_copy(src, dst, in_sem.at[n])
        for n, (src, dst) in enumerate(
            (
                (ref_hbm, ref_ref),
                (pc_hbm, pc_ref),
                (po_hbm, po_ref),
                (shift_hbm, shift_ref),
                (circle_hbm, circle_ref),
                (w_hbm, w_ref),
            )
        )
    ]
    for copy in small:
        copy.start()
    own_x.start()

    def same_core(step):
        peer_chip = lax.rem(chip + step, z.chips)
        return peer_chip, (peer_chip * 2 + core, cls)

    def same_images(step):
        peer = lax.rem(slot + step, z.group)
        return peer, (chip * 2 + lax.rem(peer, 2), peer // 2)

    barrier = pltpu.get_barrier_semaphore()

    def greet_refs(step, c):
        _, device = same_core(step)
        pl.semaphore_signal(barrier, inc=1, device_id=device, device_id_type=MESH)
        return c

    def greet_stats(step, c):
        _, device = same_images(step)
        pl.semaphore_signal(barrier, inc=1, device_id=device, device_id_type=MESH)
        return c

    lax.fori_loop(1, z.chips, greet_refs, 0)
    lax.fori_loop(1, z.group, greet_stats, 0)

    for copy in small:
        copy.wait()

    for tile in range(2 * z.tiles):
        part, kt = divmod(tile, z.tiles)
        s, k = divmod(kt, z.per_chunk)
        start = s * z.block + part * z.half_rows + k
        ref_rows[pl.ds(start, z.orient, stride=z.row_stride), :] = ref_ref[
            0, :, tile * LANES : (tile + 1) * LANES
        ].astype(F32)
    for s in range(z.chunks):
        rows = ref_rows[s * z.block : (s + 1) * z.block, :].astype(BF16)
        ref_send[s] = rows
        ref_recv[chip, s] = rows
    for i in range(z.parts):
        value = (pc_ref[i] * z.orient_all + po_ref[i]).astype(F32)
        prior[core, i : i + 1, :] = jnp.full((1, LANES), value, F32)

    pl.semaphore_wait(barrier, z.chips - 1 + z.group - 1)

    def pair_copies():
        device = (chip * 2 + other, cls)
        return (
            pltpu.make_async_remote_copy(
                src_ref=x_hbm,
                dst_ref=xb.at[core],
                send_sem=pair_send.at[0],
                recv_sem=pair_recv.at[0],
                device_id=device,
                device_id_type=MESH,
            ),
            pltpu.make_async_remote_copy(
                src_ref=prior.at[core],
                dst_ref=prior.at[core],
                send_sem=pair_send.at[1],
                recv_sem=pair_recv.at[1],
                device_id=device,
                device_id_type=MESH,
            ),
        )

    pair = pair_copies()
    for copy in pair:
        copy.start()

    def ref_copy(s, step):
        peer, device = same_core(step)
        return peer, pltpu.make_async_remote_copy(
            src_ref=ref_send.at[s],
            dst_ref=ref_recv.at[chip, s],
            send_sem=ref_ssem.at[step, s],
            recv_sem=ref_rsem.at[chip, s],
            device_id=device,
            device_id_type=MESH,
        )

    def ref_arrival(s, step):
        peer, device = same_core(step)
        return pltpu.make_async_remote_copy(
            src_ref=ref_send.at[s],
            dst_ref=ref_recv.at[peer, s],
            send_sem=ref_ssem.at[step, s],
            recv_sem=ref_rsem.at[peer, s],
            device_id=device,
            device_id_type=MESH,
        )

    def send_refs(s, c):
        def to_peer(step, c):
            ref_copy(s, step)[1].start()
            return c

        return lax.fori_loop(1, z.chips, to_peer, c)

    lax.fori_loop(0, z.chunks, send_refs, 0)

    lane = lax.broadcasted_iota(jnp.int32, (1, LANES), 1)
    half_width = L // 2 + 1

    def look_up(turn):
        turn = turn.astype(jnp.int32) & (L - 1)
        return tuple(
            jnp.take_along_axis(
                jnp.broadcast_to(ref[...], (8, LANES)), turn, axis=1, mode="promise_in_bounds"
            )
            for ref in (circle_ref.at[0:1], circle_ref.at[1:2])
        )

    lane8 = lax.broadcasted_iota(jnp.int32, (8, LANES), 1)
    sub8 = lax.broadcasted_iota(jnp.int32, (8, LANES), 0)
    shift_rows = shift_ref[...].astype(F32)
    first_row = jnp.where(lane8 >= half_width, 1, 0)
    first_col = lane8 - half_width * first_row
    rows_on, rows_over = divmod(LANES, half_width)
    rows_on, rows_back = rows_on + 1, half_width - rows_over
    span = 8
    for t0 in range(0, LANES, 8 * span):
        start, turns = [], []
        for v in range(span):
            rows = slice(t0 + 8 * v, t0 + 8 * v + 8)
            here = lane8 - sub8 == rows.start
            shift_x, shift_y = (
                jnp.broadcast_to(
                    jnp.sum(
                        jnp.where(here, jnp.broadcast_to(shift_rows[n : n + 1, :], (8, LANES)), 0.0),
                        axis=1,
                        keepdims=True,
                    ),
                    (8, LANES),
                )
                for n in range(2)
            )
            start.append(
                look_up(first_col.astype(F32) * shift_x + first_row.astype(F32) * shift_y)
            )
            turns.append(
                (
                    look_up(rows_on * shift_y - rows_back * shift_x),
                    look_up((rows_on - 1) * shift_y + rows_over * shift_x),
                )
            )

        def make_table(step, carry):
            now, col = carry
            for j in range(z.per_chunk):
                kt = step * z.per_chunk + j
                near = col >= rows_back
                col = jnp.where(near, col - rows_back, col + rows_over)
                after = []
                for v in range(span):
                    cosine, sine = now[v]
                    rows = slice(t0 + 8 * v, t0 + 8 * v + 8)
                    tab[kt, rows, :LANES] = cosine.astype(BF16)
                    tab[kt, rows, LANES:] = sine.astype(BF16)
                    turn_cos = jnp.where(near, turns[v][0][0], turns[v][1][0])
                    turn_sin = jnp.where(near, turns[v][0][1], turns[v][1][1])
                    after.append(
                        (
                            cosine * turn_cos - sine * turn_sin,
                            sine * turn_cos + cosine * turn_sin,
                        )
                    )
                now = tuple(after)
            return now, col

        lax.fori_loop(0, z.chunks, make_table, (tuple(start), first_col))

    own_x.wait()
    for copy in pair:
        copy.wait_recv()

    def widen(tile, c):
        at = pl.multiple_of(tile * LANES, LANES)
        to = pl.multiple_of(tile * z.imgs, 8)
        for half in range(2):
            x32[pl.ds(to + half * z.parts, z.parts), :] = xb[half, :, pl.ds(at, LANES)].astype(F32)
        return c

    lax.fori_loop(0, 2 * z.tiles, widen, 0)

    def image_row(tile, i):
        return x32[pl.ds(tile * z.imgs + i, 8, stride=0), :]

    halves = z.refs // 8
    acc[...] = jnp.zeros_like(acc)
    power[...] = jnp.zeros_like(power)

    def score_chunk(s, c):
        def arrive(step, c):
            ref_arrival(s, step).wait_recv()
            return c

        lax.fori_loop(1, z.chips, arrive, 0)
        for peer in range(z.chips):
            ref_f32[peer * z.block : (peer + 1) * z.block, :] = ref_recv[peer, s].astype(F32)

        def tile_step(k):
            kt = s * z.per_chunk + k
            noise = w_ref[pl.ds(kt, 8, stride=0), :]
            real, imag = [], []
            for h in range(halves):
                first = h * 8 * z.row_stride + k
                a_real = ref_f32[pl.ds(first, 8, stride=z.row_stride), :]
                a_imag = ref_f32[pl.ds(first + z.half_rows, 8, stride=z.row_stride), :]
                w_real = noise * a_real
                w_imag = noise * a_imag
                power[h * 8 : (h + 1) * 8, :] += w_real * a_real + w_imag * a_imag
                real.append(w_real)
                imag.append(w_imag)
            lhs = []
            for i in range(z.imgs):
                x_real = image_row(kt, i)
                x_imag = image_row(z.tiles + kt, i)
                p_real = jnp.concatenate(
                    [real[h] * x_real + imag[h] * x_imag for h in range(halves)], 0
                )
                p_imag = jnp.concatenate(
                    [real[h] * x_imag - imag[h] * x_real for h in range(halves)], 0
                )
                lhs.append(jnp.concatenate([p_real.astype(BF16), p_imag.astype(BF16)], 1))
            acc[...] += lax.dot_general(
                jnp.concatenate(lhs, 0),
                tab[kt],
                (((1,), (1,)), ((), ())),
                preferred_element_type=F32,
            )

        for k in range(z.per_chunk):
            tile_step(k)
        return c

    lax.fori_loop(0, z.chunks, score_chunk, 0)

    row = lax.broadcasted_iota(jnp.int32, (z.refs, LANES), 0)
    class_id = 2 * (row // z.orient) + core
    ref_id = class_id * z.orient_all + cls * z.orient + lax.rem(row, z.orient)
    ref_id = ref_id.astype(F32)
    half_power = 0.5 * jnp.sum(power[...], axis=1, keepdims=True)
    for i in range(z.imgs):
        half, il = divmod(i, z.parts)
        block = acc[i * z.refs : (i + 1) * z.refs, :] - half_power
        block = block + jnp.where(prior[half, il : il + 1, :] == ref_id, PRIOR_LOG_BOOST, 0.0)
        acc[i * z.refs : (i + 1) * z.refs, :] = block
        top[i : i + 1, :] = jnp.max(block, axis=0, keepdims=True)
    top[...] = jnp.broadcast_to(jnp.max(top[...], axis=1, keepdims=True), top.shape)
    for i in range(z.imgs):
        block = jnp.exp(acc[i * z.refs : (i + 1) * z.refs, :] - top[i : i + 1, :])
        acc[i * z.refs : (i + 1) * z.refs, :] = block
        total[i : i + 1, :] = jnp.sum(block, axis=0, keepdims=True)
    sums = jnp.sum(total[...], axis=1, keepdims=True)
    groups = z.imgs // 8
    packed = jnp.zeros((8, LANES), F32)
    for v in range(groups):
        packed = jnp.where(lane8 == v, top[v * 8 : (v + 1) * 8, :], packed)
        packed = jnp.where(lane8 == groups + v, sums[v * 8 : (v + 1) * 8, :], packed)
    stats[slot] = packed

    def stat_copy(step):
        _, device = same_images(step)
        return pltpu.make_async_remote_copy(
            src_ref=stats.at[slot],
            dst_ref=stats.at[slot],
            send_sem=stat_ssem.at[step],
            recv_sem=stat_rsem.at[slot],
            device_id=device,
            device_id_type=MESH,
        )

    def stat_arrival(step):
        peer, device = same_images(step)
        return pltpu.make_async_remote_copy(
            src_ref=stats.at[peer],
            dst_ref=stats.at[peer],
            send_sem=stat_ssem.at[step],
            recv_sem=stat_rsem.at[peer],
            device_id=device,
            device_id_type=MESH,
        )

    def send_stat(step, c):
        stat_copy(step).start()
        return c

    def take_stat(step, c):
        stat_arrival(step).wait_recv()
        return c

    lax.fori_loop(1, z.group, send_stat, 0)
    lax.fori_loop(1, z.group, take_stat, 0)

    all_top = stats[0]
    for g in range(1, z.group):
        all_top = jnp.maximum(all_top, stats[g])
    all_total = jnp.zeros((8, LANES), F32)
    for g in range(z.group):
        part = stats[g]
        all_total = all_total + jnp.exp(part - all_top) * pltpu.roll(part, LANES - groups, 1)
    log_norm = all_top + jnp.log(all_total)
    rescale = jnp.exp(packed - log_norm)
    for v in range(groups):
        scale[v * 8 : (v + 1) * 8, :] = jnp.broadcast_to(rescale[:, v : v + 1], (8, LANES))
        total[v * 8 : (v + 1) * 8, :] = jnp.broadcast_to(log_norm[:, v : v + 1], (8, LANES))
    mine = total[pl.ds(pl.multiple_of(core * z.parts, 8), z.parts), :]
    diagonal = lax.broadcasted_iota(jnp.int32, (z.parts, LANES), 0) == lax.broadcasted_iota(
        jnp.int32, (z.parts, LANES), 1
    )
    ln_ref[...] = jnp.sum(jnp.where(diagonal, mine, 0.0), axis=0, keepdims=True)

    mass = jnp.zeros((z.refs, LANES), F32)
    for i in range(z.imgs):
        block = acc[i * z.refs : (i + 1) * z.refs, :] * scale[i : i + 1, :]
        mass = mass + block
        post[i * z.refs : (i + 1) * z.refs, :] = block.astype(BF16)
    weight[...] = jnp.broadcast_to(jnp.sum(mass, axis=1, keepdims=True), weight.shape)

    def back_copy(s, step):
        peer, device = same_core(step)
        return pltpu.make_async_remote_copy(
            src_ref=back_send.at[peer, s],
            dst_ref=back_recv.at[chip, s],
            send_sem=back_ssem.at[step, s],
            recv_sem=back_rsem.at[chip, s],
            device_id=device,
            device_id_type=MESH,
        )

    def back_arrival(s, step):
        peer, device = same_core(step)
        return pltpu.make_async_remote_copy(
            src_ref=back_send.at[peer, s],
            dst_ref=back_recv.at[peer, s],
            send_sem=back_ssem.at[step, s],
            recv_sem=back_rsem.at[peer, s],
            device_id=device,
            device_id_type=MESH,
        )

    def back_chunk(s, c):
        def tile_step(k):
            kt = s * z.per_chunk + k
            coeff = jnp.dot(post[...], tab[kt], preferred_element_type=F32)
            real = [jnp.zeros((8, LANES), F32) for _ in range(halves)]
            imag = [jnp.zeros((8, LANES), F32) for _ in range(halves)]
            for i in range(z.imgs):
                x_real = image_row(kt, i)
                x_imag = image_row(z.tiles + kt, i)
                for h in range(halves):
                    at = i * z.refs + h * 8
                    cosine = coeff[at : at + 8, :LANES]
                    sine = coeff[at : at + 8, LANES:]
                    real[h] = real[h] + (x_real * cosine + x_imag * sine)
                    imag[h] = imag[h] + (x_imag * cosine - x_real * sine)
            for h in range(halves):
                first = h * 8 * z.row_stride + k
                back_rows[pl.ds(first, 8, stride=z.row_stride), :] = real[h]
                back_rows[pl.ds(first + z.half_rows, 8, stride=z.row_stride), :] = imag[h]

        for k in range(z.per_chunk):
            tile_step(k)
        high = weight[...].astype(BF16).astype(F32)
        low = weight[...] - high
        for h in range(halves):
            first = h * 8 * z.row_stride + z.per_chunk
            rows = slice(h * 8, (h + 1) * 8)
            back_rows[pl.ds(first, 8, stride=z.row_stride), :] = high[rows]
            back_rows[pl.ds(first + z.half_rows, 8, stride=z.row_stride), :] = low[rows]
        for peer in range(z.chips):
            back_send[peer, s] = back_rows[peer * z.block : (peer + 1) * z.block, :].astype(BF16)
        back_own[s] = back_rows[pl.ds(pl.multiple_of(chip * z.block, 8), z.block), :]

        def to_peer(step, c):
            back_copy(s, step).start()
            return c

        return lax.fori_loop(1, z.chips, to_peer, c)

    lax.fori_loop(0, z.chunks, back_chunk, 0)

    def gather_chunk(s, c):
        def arrive(step, c):
            back_arrival(s, step).wait_recv()
            return c

        lax.fori_loop(1, z.chips, arrive, 0)

        def add(step, got):
            peer, _ = same_core(step)
            return got + back_recv[peer, s].astype(F32)

        sum_ref[pl.ds(pl.multiple_of(s * z.block, 8), z.block), :] = lax.fori_loop(
            1, z.chips, add, back_own[s]
        )
        return c

    lax.fori_loop(0, z.chunks, gather_chunk, 0)
    for copy in pair:
        copy.wait_send()

    def drain_chunk(s, c):
        def drain(step, c):
            ref_copy(s, step)[1].wait_send()
            back_copy(s, step).wait_send()
            return c

        return lax.fori_loop(1, z.chips, drain, c)

    def drain_stat(step, c):
        stat_copy(step).wait_send()
        return c

    lax.fori_loop(0, z.chunks, drain_chunk, 0)
    lax.fori_loop(1, z.group, drain_stat, 0)


def finish(z, sum_ref, ln_ref, bp_ref, cw_ref, lnorm_ref, bp_buf, cw_buf, ln_buf, sem):
    lane = lax.broadcasted_iota(jnp.int32, (1, LANES), 1)
    for tile in range(2 * z.tiles):
        part, kt = divmod(tile, z.tiles)
        s, k = divmod(kt, z.per_chunk)
        start = s * z.block + part * z.half_rows + k
        bp_buf[0, :, tile * LANES : (tile + 1) * LANES] = sum_ref[
            pl.ds(start, z.orient, stride=z.row_stride), :
        ]
    line = jnp.zeros((1, LANES), F32)
    for o in range(z.orient):
        at = o * z.row_stride + z.per_chunk
        both = sum_ref[at : at + 1, :] + sum_ref[at + z.half_rows : at + z.half_rows + 1, :]
        line = jnp.where(lane == o, both, line)
    cw_buf[...] = line[:, : z.orient]

    ln_buf[...] = ln_ref[:, : z.parts]
    copies = [
        pltpu.make_async_copy(src, dst, sem.at[n])
        for n, (src, dst) in enumerate(
            ((bp_buf, bp_ref), (cw_buf, cw_ref), (ln_buf, lnorm_ref))
        )
    ]
    for copy in copies:
        copy.start()
    for copy in copies:
        copy.wait()


def on_device(z, particles, references, inv_noise, shifts, prior_class, prior_orient):
    angle = (np.arange(L, dtype=np.float32) * np.float32(2.0 * math.pi / L)).astype(np.float64)
    circle = jnp.asarray(np.stack([np.cos(angle), np.sin(angle)]).astype(np.float32))
    vmem = pl.BlockSpec(memory_space=pltpu.VMEM)
    hbm = pl.BlockSpec(memory_space=pltpu.HBM)
    dma = pltpu.SemaphoreType.DMA
    blocks = (z.chips, z.chunks, z.block, LANES)
    flops = 4 * z.rows * z.feat * LANES
    sums, ln_row = pl.pallas_call(
        functools.partial(kernel, z),
        out_shape=(
            jax.ShapeDtypeStruct((z.chunks * z.block, LANES), F32),
            jax.ShapeDtypeStruct((1, LANES), F32),
        ),
        in_specs=[hbm] * 7,
        out_specs=(vmem, vmem),
        scratch_shapes=[
            pltpu.VMEM((1, z.orient, z.feat), BF16),
            pltpu.VMEM((z.tiles, LANES), F32),
            pltpu.VMEM((2, LANES), jnp.int32),
            pltpu.SMEM((z.parts,), jnp.int32),
            pltpu.SMEM((z.parts,), jnp.int32),
            pltpu.VMEM((2, LANES), F32),
            pltpu.VMEM((2, z.parts, z.feat), BF16),
            pltpu.VMEM((2 * z.tiles * z.imgs, LANES), F32),
            pltpu.VMEM((z.tiles, LANES, 2 * LANES), BF16),
            pltpu.VMEM((2, z.parts, LANES), F32),
            pltpu.VMEM((z.chunks * z.block, LANES), F32),
            pltpu.VMEM((z.chunks, z.block, LANES), BF16),
            pltpu.VMEM(blocks, BF16),
            pltpu.VMEM((z.chips * z.block, LANES), F32),
            pltpu.VMEM((z.rows, LANES), F32),
            pltpu.VMEM((z.refs, LANES), F32),
            pltpu.VMEM((z.imgs, LANES), F32),
            pltpu.VMEM((z.imgs, LANES), F32),
            pltpu.VMEM((z.group, 8, LANES), F32),
            pltpu.VMEM((z.imgs, LANES), F32),
            pltpu.VMEM((z.rows, LANES), BF16),
            pltpu.VMEM((z.refs, LANES), F32),
            pltpu.VMEM((z.chips * z.block, LANES), F32),
            pltpu.VMEM(blocks, BF16),
            pltpu.VMEM(blocks, BF16),
            pltpu.VMEM((z.chunks, z.block, LANES), F32),
            dma,
            dma((6,)),
            dma((2,)),
            dma((2,)),
            dma((z.chips, z.chunks)),
            dma((z.chips, z.chunks)),
            dma((z.group,)),
            dma((z.group,)),
            dma((z.chips, z.chunks)),
            dma((z.chips, z.chunks)),
        ],
        compiler_params=pltpu.CompilerParams(
            collective_id=0, has_side_effects=True, vmem_limit_bytes=65536 * 2**10
        ),
        cost_estimate=pl.CostEstimate(
            flops=flops, bytes_accessed=4 * 2**20, transcendentals=z.rows * LANES
        ),
    )(
        particles,
        references,
        inv_noise.reshape(z.tiles, LANES),
        shifts.T,
        prior_class,
        prior_orient,
        circle,
    )
    bp, cw, ln = pl.pallas_call(
        functools.partial(finish, z),
        out_shape=(
            jax.ShapeDtypeStruct((1, z.orient, z.feat), F32),
            jax.ShapeDtypeStruct((1, z.orient), F32),
            jax.ShapeDtypeStruct((1, z.parts), F32),
        ),
        in_specs=[vmem, vmem],
        out_specs=(hbm, hbm, hbm),
        scratch_shapes=[
            pltpu.VMEM((1, z.orient, z.feat), F32),
            pltpu.VMEM((1, z.orient), F32),
            pltpu.VMEM((1, z.parts), F32),
            dma((3,)),
        ],
    )(sums, ln_row)
    return bp, cw, ln.reshape(z.parts)


def solution(mesh):
    def body(particles, references, inv_noise, shifts, prior_class, prior_orient):
        n_dom, n_cls = lax.axis_size("dom"), lax.axis_size("cls")
        z = Sizes(
            n_dom,
            n_cls,
            particles.shape[0],
            references.shape[1],
            particles.shape[1],
            references.shape[1] * n_cls,
        )
        return on_device(z, particles, references, inv_noise, shifts, prior_class, prior_orient)

    placed = (P("dom", None), P("dom", "cls", None), P(), P(), P("dom"), P("dom"))
    return jax.shard_map(
        body,
        mesh=mesh,
        in_specs=placed,
        out_specs=(P("dom", "cls", None), P("dom", "cls"), P("dom")),
        check_vma=False,
    )
```

```python
import functools
import math

import jax
import jax.numpy as jnp
import numpy as np
from jax import lax
from jax.experimental import pallas as pl
from jax.experimental.pallas import tpu as pltpu
from jax.sharding import PartitionSpec as P

L = 128
LANES = 128
PRIOR_LOG_BOOST = 12.0
MESH = pl.DeviceIdType.MESH
F32 = jnp.float32
BF16 = jnp.bfloat16


class Run:
    def __init__(self, n, first, count, half, orient):
        self.n = n
        self.first = first
        self.count = count
        self.half = half
        self.stride = 2 * half
        self.block = orient * self.stride


class Sizes:
    def __init__(self, n_dom, n_cls, parts, orient, feat):
        self.chips = n_dom // 2
        self.n_cls = n_cls
        self.parts = parts
        self.orient = orient
        self.orient_all = orient * n_cls
        self.feat = feat
        self.tiles = feat // 2 // LANES
        n = 14
        count = self.tiles // n
        left = self.tiles - n * count
        self.lead = Run(left, 0, 1, left + 1, orient)
        self.bulk = Run(n, left, count, n, orient)
        self.runs = (self.lead, self.bulk)
        self.refs = self.chips * orient
        self.imgs = 2 * parts
        self.rows = self.imgs * self.refs
        self.group = 2 * n_cls


class Bufs:
    def __init__(
        self,
        run,
        rows,
        send,
        recv,
        wide,
        back,
        back_send,
        back_recv,
        back_own,
        ssem,
        rsem,
        back_ssem,
        back_rsem,
    ):
        self.run = run
        self.rows = rows
        self.send = send
        self.recv = recv
        self.wide = wide
        self.back = back
        self.back_send = back_send
        self.back_recv = back_recv
        self.back_own = back_own
        self.ssem = ssem
        self.rsem = rsem
        self.back_ssem = back_ssem
        self.back_rsem = back_rsem


def place(z, tile):
    part, kt = divmod(tile, z.tiles)
    if kt < z.lead.n:
        return 0, 0, part * z.lead.half + kt
    s, k = divmod(kt - z.lead.n, z.bulk.n)
    return 1, s, part * z.bulk.half + k


def kernel(
    z,
    x_hbm,
    ref_hbm,
    w_hbm,
    shift_hbm,
    pc_hbm,
    po_hbm,
    circle_hbm,
    bp_ref,
    cw_ref,
    ln_ref,
    ref_ref,
    w_ref,
    shift_ref,
    pc_ref,
    po_ref,
    circle_ref,
    xb,
    x32,
    tab,
    prior,
    acc,
    power,
    top,
    total,
    stats,
    scale,
    post,
    weight,
    x_sem,
    in_sem,
    pair_send,
    pair_recv,
    stat_ssem,
    stat_rsem,
    *per_run,
):
    size = len(per_run) // 2
    runs = [Bufs(r, *per_run[n * size : (n + 1) * size]) for n, r in enumerate(z.runs)]
    lead, bulk = runs
    dom = lax.axis_index("dom")
    cls = lax.axis_index("cls")
    chip = dom // 2
    core = lax.rem(dom, 2)
    slot = cls * 2 + core
    other = 1 - core

    own_x = pltpu.make_async_copy(x_hbm, xb.at[core], x_sem)
    small = [
        pltpu.make_async_copy(src, dst, in_sem.at[n])
        for n, (src, dst) in enumerate(
            (
                (ref_hbm, ref_ref),
                (pc_hbm, pc_ref),
                (po_hbm, po_ref),
                (shift_hbm, shift_ref),
                (circle_hbm, circle_ref),
                (w_hbm, w_ref),
            )
        )
    ]
    def wait_all(like, sem):
        pltpu.make_async_copy(like, like, sem).wait()

    def same_core(step):
        peer_chip = lax.rem(chip + step, z.chips)
        return peer_chip, (peer_chip * 2 + core, cls)

    def same_images(step):
        peer = lax.rem(slot + step, z.group)
        return peer, (chip * 2 + lax.rem(peer, 2), peer // 2)

    barrier = pltpu.get_barrier_semaphore()

    def greet_refs(step, c):
        _, device = same_core(step)
        pl.semaphore_signal(barrier, inc=1, device_id=device, device_id_type=MESH)
        return c

    def greet_stats(step, c):
        _, device = same_images(step)
        pl.semaphore_signal(barrier, inc=1, device_id=device, device_id_type=MESH)
        return c

    lax.fori_loop(1, z.chips, greet_refs, 0)
    lax.fori_loop(1, z.group, greet_stats, 0)

    for copy in small:
        copy.start()
    own_x.start()

    for copy in small:
        copy.wait()

    for tile in range(2 * z.tiles):
        n, s, row = place(z, tile)
        start = s * z.runs[n].block + row
        runs[n].rows[pl.ds(start, z.orient, stride=z.runs[n].stride), :] = ref_ref[
            0, :, tile * LANES : (tile + 1) * LANES
        ].astype(F32)
    for b in runs:
        for s in range(b.run.count):
            rows = b.rows[s * b.run.block : (s + 1) * b.run.block, :].astype(BF16)
            b.send[s] = rows
            b.recv[chip, s] = rows
    pl.semaphore_wait(barrier, z.chips - 1 + z.group - 1)

    def pair_copies():
        device = (chip * 2 + other, cls)
        return (
            pltpu.make_async_remote_copy(
                src_ref=x_hbm,
                dst_ref=xb.at[core],
                send_sem=pair_send.at[0],
                recv_sem=pair_recv.at[0],
                device_id=device,
                device_id_type=MESH,
            ),
            pltpu.make_async_remote_copy(
                src_ref=prior.at[core],
                dst_ref=prior.at[core],
                send_sem=pair_send.at[1],
                recv_sem=pair_recv.at[1],
                device_id=device,
                device_id_type=MESH,
            ),
        )

    pair = pair_copies()
    def ref_copy(b, s, step):
        _, device = same_core(step)
        return pltpu.make_async_remote_copy(
            src_ref=b.send.at[s],
            dst_ref=b.recv.at[chip, s],
            send_sem=b.ssem,
            recv_sem=b.rsem.at[s],
            device_id=device,
            device_id_type=MESH,
        )

    for b in runs:

        def send_refs(s, c, b=b):
            def to_peer(step, c):
                ref_copy(b, s, step).start()
                return c

            return lax.fori_loop(1, z.chips, to_peer, c)

        lax.fori_loop(0, b.run.count, send_refs, 0)
        if b is lead:
            pair[0].start()

    for i in range(z.parts):
        value = (pc_ref[i] * z.orient_all + po_ref[i]).astype(F32)
        prior[core, i : i + 1, :] = jnp.full((1, LANES), value, F32)
    pair[1].start()

    lane = lax.broadcasted_iota(jnp.int32, (1, LANES), 1)
    half_width = L // 2 + 1

    def look_up(turn):
        turn = turn.astype(jnp.int32) & (L - 1)
        return tuple(
            jnp.take_along_axis(
                jnp.broadcast_to(ref[...], (8, LANES)), turn, axis=1, mode="promise_in_bounds"
            )
            for ref in (circle_ref.at[0:1], circle_ref.at[1:2])
        )

    lane8 = lax.broadcasted_iota(jnp.int32, (8, LANES), 1)
    sub8 = lax.broadcasted_iota(jnp.int32, (8, LANES), 0)
    shift_rows = shift_ref[...].astype(F32)
    first_row = jnp.where(lane8 >= half_width, 1, 0)
    first_col = lane8 - half_width * first_row
    rows_on, rows_over = divmod(LANES, half_width)
    rows_on, rows_back = rows_on + 1, half_width - rows_over
    span = 8
    unroll = 13 if z.tiles % 13 == 0 else 1
    for t0 in range(0, LANES, 8 * span):
        start, turns = [], []
        for v in range(span):
            rows = slice(t0 + 8 * v, t0 + 8 * v + 8)
            here = lane8 - sub8 == rows.start
            shift_x, shift_y = (
                jnp.broadcast_to(
                    jnp.sum(
                        jnp.where(here, jnp.broadcast_to(shift_rows[n : n + 1, :], (8, LANES)), 0.0),
                        axis=1,
                        keepdims=True,
                    ),
                    (8, LANES),
                )
                for n in range(2)
            )
            start.append(
                look_up(first_col.astype(F32) * shift_x + first_row.astype(F32) * shift_y)
            )
            turns.append(
                (
                    look_up(rows_on * shift_y - rows_back * shift_x),
                    look_up((rows_on - 1) * shift_y + rows_over * shift_x),
                )
            )

        def make_table(step, carry):
            now, col = carry
            for j in range(unroll):
                kt = step * unroll + j
                near = col >= rows_back
                col = jnp.where(near, col - rows_back, col + rows_over)
                after = []
                for v in range(span):
                    cosine, sine = now[v]
                    rows = slice(t0 + 8 * v, t0 + 8 * v + 8)
                    tab[kt, rows, :LANES] = cosine.astype(BF16)
                    tab[kt, rows, LANES:] = sine.astype(BF16)
                    turn_cos = jnp.where(near, turns[v][0][0], turns[v][1][0])
                    turn_sin = jnp.where(near, turns[v][0][1], turns[v][1][1])
                    after.append(
                        (
                            cosine * turn_cos - sine * turn_sin,
                            sine * turn_cos + cosine * turn_sin,
                        )
                    )
                now = tuple(after)
            return now, col

        lax.fori_loop(0, z.tiles // unroll, make_table, (tuple(start), first_col))

    own_x.wait()
    for copy in pair:
        copy.wait_recv()

    def widen(tile, c):
        at = pl.multiple_of(tile * LANES, LANES)
        to = pl.multiple_of(tile * z.imgs, 8)
        for half in range(2):
            x32[pl.ds(to + half * z.parts, z.parts), :] = xb[half, :, pl.ds(at, LANES)].astype(F32)
        return c

    lax.fori_loop(0, 2 * z.tiles, widen, 0)

    def image_row(tile, i):
        return x32[pl.ds(tile * z.imgs + i, 8, stride=0), :]

    halves = z.refs // 8
    acc[...] = jnp.zeros_like(acc)
    power[...] = jnp.zeros_like(power)

    def score_chunk(b, s):
        run = b.run

        wait_all(b.recv.at[pl.ds(0, z.chips - 1), s], b.rsem.at[s])
        for peer in range(z.chips):
            b.wide[peer * run.block : (peer + 1) * run.block, :] = b.recv[peer, s].astype(F32)

        def tile_step(k):
            kt = run.first + s * run.n + k
            noise = w_ref[pl.ds(kt, 8, stride=0), :]
            real, imag = [], []
            for h in range(halves):
                first = h * 8 * run.stride + k
                a_real = b.wide[pl.ds(first, 8, stride=run.stride), :]
                a_imag = b.wide[pl.ds(first + run.half, 8, stride=run.stride), :]
                w_real = noise * a_real
                w_imag = noise * a_imag
                power[h * 8 : (h + 1) * 8, :] += w_real * a_real + w_imag * a_imag
                real.append(w_real)
                imag.append(w_imag)
            lhs = []
            for i in range(z.imgs):
                x_real = image_row(kt, i)
                x_imag = image_row(z.tiles + kt, i)
                p_real = jnp.concatenate(
                    [real[h] * x_real + imag[h] * x_imag for h in range(halves)], 0
                )
                p_imag = jnp.concatenate(
                    [real[h] * x_imag - imag[h] * x_real for h in range(halves)], 0
                )
                lhs.append(jnp.concatenate([p_real.astype(BF16), p_imag.astype(BF16)], 1))
            acc[...] += lax.dot_general(
                jnp.concatenate(lhs, 0),
                tab[kt],
                (((1,), (1,)), ((), ())),
                preferred_element_type=F32,
            )

        for k in range(run.n):
            tile_step(k)

    def score_bulk(s, c):
        score_chunk(bulk, s)
        return c

    score_chunk(lead, 0)
    lax.fori_loop(0, bulk.run.count, score_bulk, 0)

    row = lax.broadcasted_iota(jnp.int32, (z.refs, LANES), 0)
    class_id = 2 * (row // z.orient) + core
    ref_id = class_id * z.orient_all + cls * z.orient + lax.rem(row, z.orient)
    ref_id = ref_id.astype(F32)
    half_power = 0.5 * jnp.sum(power[...], axis=1, keepdims=True)
    for i in range(z.imgs):
        half, il = divmod(i, z.parts)
        block = acc[i * z.refs : (i + 1) * z.refs, :] - half_power
        block = block + jnp.where(prior[half, il : il + 1, :] == ref_id, PRIOR_LOG_BOOST, 0.0)
        acc[i * z.refs : (i + 1) * z.refs, :] = block
        top[i : i + 1, :] = jnp.max(block, axis=0, keepdims=True)
    top[...] = jnp.broadcast_to(jnp.max(top[...], axis=1, keepdims=True), top.shape)
    for i in range(z.imgs):
        block = jnp.exp(acc[i * z.refs : (i + 1) * z.refs, :] - top[i : i + 1, :])
        acc[i * z.refs : (i + 1) * z.refs, :] = block
        total[i : i + 1, :] = jnp.sum(block, axis=0, keepdims=True)
    sums = jnp.sum(total[...], axis=1, keepdims=True)
    groups = z.imgs // 8
    packed = jnp.zeros((8, LANES), F32)
    for v in range(groups):
        packed = jnp.where(lane8 == v, top[v * 8 : (v + 1) * 8, :], packed)
        packed = jnp.where(lane8 == groups + v, sums[v * 8 : (v + 1) * 8, :], packed)
    stats[slot] = packed

    def stat_copy(step):
        _, device = same_images(step)
        return pltpu.make_async_remote_copy(
            src_ref=stats.at[slot],
            dst_ref=stats.at[slot],
            send_sem=stat_ssem,
            recv_sem=stat_rsem,
            device_id=device,
            device_id_type=MESH,
        )

    def send_stat(step, c):
        stat_copy(step).start()
        return c

    lax.fori_loop(1, z.group, send_stat, 0)
    wait_all(stats.at[pl.ds(0, z.group - 1)], stat_rsem)

    all_top = stats[0]
    for g in range(1, z.group):
        all_top = jnp.maximum(all_top, stats[g])
    all_total = jnp.zeros((8, LANES), F32)
    for g in range(z.group):
        part = stats[g]
        all_total = all_total + jnp.exp(part - all_top) * pltpu.roll(part, LANES - groups, 1)
    log_norm = all_top + jnp.log(all_total)
    rescale = jnp.exp(packed - log_norm)
    for v in range(groups):
        scale[v * 8 : (v + 1) * 8, :] = jnp.broadcast_to(rescale[:, v : v + 1], (8, LANES))
        total[v * 8 : (v + 1) * 8, :] = jnp.broadcast_to(log_norm[:, v : v + 1], (8, LANES))
    mass = jnp.zeros((z.refs, LANES), F32)
    for i in range(z.imgs):
        block = acc[i * z.refs : (i + 1) * z.refs, :] * scale[i : i + 1, :]
        mass = mass + block
        post[i * z.refs : (i + 1) * z.refs, :] = block.astype(BF16)
    weight[...] = jnp.broadcast_to(jnp.sum(mass, axis=1, keepdims=True), weight.shape)

    def back_copy(b, s, step):
        peer, device = same_core(step)
        return pltpu.make_async_remote_copy(
            src_ref=b.back_send.at[peer, s],
            dst_ref=b.back_recv.at[chip, s],
            send_sem=b.back_ssem,
            recv_sem=b.back_rsem.at[s],
            device_id=device,
            device_id_type=MESH,
        )

    def back_chunk(b, s):
        run = b.run

        def tile_step(k):
            kt = run.first + s * run.n + k
            coeff = jnp.dot(post[...], tab[kt], preferred_element_type=F32)
            real = [jnp.zeros((8, LANES), F32) for _ in range(halves)]
            imag = [jnp.zeros((8, LANES), F32) for _ in range(halves)]
            for i in range(z.imgs):
                x_real = image_row(kt, i)
                x_imag = image_row(z.tiles + kt, i)
                for h in range(halves):
                    at = i * z.refs + h * 8
                    cosine = coeff[at : at + 8, :LANES]
                    sine = coeff[at : at + 8, LANES:]
                    real[h] = real[h] + (x_real * cosine + x_imag * sine)
                    imag[h] = imag[h] + (x_imag * cosine - x_real * sine)
            for h in range(halves):
                first = h * 8 * run.stride + k
                b.back[pl.ds(first, 8, stride=run.stride), :] = real[h]
                b.back[pl.ds(first + run.half, 8, stride=run.stride), :] = imag[h]

        for k in range(run.n):
            tile_step(k)
        if run.half > run.n:
            high = weight[...].astype(BF16).astype(F32)
            low = weight[...] - high
            for h in range(halves):
                first = h * 8 * run.stride + run.n
                rows = slice(h * 8, (h + 1) * 8)
                b.back[pl.ds(first, 8, stride=run.stride), :] = high[rows]
                b.back[pl.ds(first + run.half, 8, stride=run.stride), :] = low[rows]
        for peer in range(z.chips):
            b.back_send[peer, s] = b.back[peer * run.block : (peer + 1) * run.block, :].astype(BF16)
        b.back_own[s] = b.back[pl.ds(pl.multiple_of(chip * run.block, 8), run.block), :]

        def to_peer(step, c):
            back_copy(b, s, step).start()
            return c

        lax.fori_loop(1, z.chips, to_peer, 0)

    def back_bulk(s, c):
        back_chunk(bulk, s)
        return c

    lax.fori_loop(0, bulk.run.count, back_bulk, 0)
    back_chunk(lead, 0)

    for copy in pair:
        copy.wait_send()

    for b in runs:
        wait_all(b.recv.at[pl.ds(0, z.chips - 1)], b.ssem)
        wait_all(b.back_recv.at[pl.ds(0, z.chips - 1)], b.back_ssem)
    wait_all(stats.at[pl.ds(0, z.group - 1)], stat_ssem)

    mine = total[pl.ds(pl.multiple_of(core * z.parts, 8), z.parts), :]
    diagonal = lax.broadcasted_iota(jnp.int32, (z.parts, LANES), 0) == lax.broadcasted_iota(
        jnp.int32, (z.parts, LANES), 1
    )
    ln_ref[...] = jnp.sum(jnp.where(diagonal, mine, 0.0), axis=0, keepdims=True)[:, : z.parts]

    for b in (bulk, lead):
        run = b.run

        def gather_chunk(s, c, b=b):
            wait_all(b.back_recv.at[pl.ds(0, z.chips - 1), s], b.back_rsem.at[s])

            def add(step, got):
                peer, _ = same_core(step)
                return got + b.back_recv[peer, s].astype(F32)

            at = pl.multiple_of(s * b.run.block, 8)
            b.rows[pl.ds(at, b.run.block), :] = lax.fori_loop(1, z.chips, add, b.back_own[s])
            return c

        lax.fori_loop(0, run.count, gather_chunk, 0)
        for tile in range(2 * z.tiles):
            n, s, row = place(z, tile)
            if runs[n] is b:
                bp_ref[0, :, tile * LANES : (tile + 1) * LANES] = b.rows[
                    pl.ds(s * run.block + row, z.orient, stride=run.stride), :
                ]
    line = jnp.zeros((1, LANES), F32)
    for o in range(z.orient):
        at = o * lead.run.stride + lead.run.n
        low = at + lead.run.half
        line = jnp.where(lane == o, lead.rows[at : at + 1, :] + lead.rows[low : low + 1, :], line)
    cw_ref[...] = line[:, : z.orient]


def finish(bp_in, cw_in, ln_in, bp_ref, cw_ref, ln_ref, sem):
    copies = [
        pltpu.make_async_copy(src, dst, sem.at[n])
        for n, (src, dst) in enumerate(((bp_in, bp_ref), (cw_in, cw_ref), (ln_in, ln_ref)))
    ]
    for copy in copies:
        copy.start()
    for copy in copies:
        copy.wait()


def on_device(z, particles, references, inv_noise, shifts, prior_class, prior_orient):
    angle = (np.arange(L, dtype=np.float32) * np.float32(2.0 * math.pi / L)).astype(np.float64)
    circle = jnp.asarray(np.stack([np.cos(angle), np.sin(angle)]).astype(np.float32))
    vmem = pl.BlockSpec(memory_space=pltpu.VMEM)
    hbm = pl.BlockSpec(memory_space=pltpu.HBM)
    dma = pltpu.SemaphoreType.DMA
    flops = 4 * z.rows * z.feat * LANES
    per_run = []
    for run in z.runs:
        per_run += [
            pltpu.VMEM((run.count * run.block, LANES), F32),
            pltpu.VMEM((run.count, run.block, LANES), BF16),
            pltpu.VMEM((z.chips, run.count, run.block, LANES), BF16),
            pltpu.VMEM((z.chips * run.block, LANES), F32),
            pltpu.VMEM((z.chips * run.block, LANES), F32),
            pltpu.VMEM((z.chips, run.count, run.block, LANES), BF16),
            pltpu.VMEM((z.chips, run.count, run.block, LANES), BF16),
            pltpu.VMEM((run.count, run.block, LANES), F32),
            dma,
            dma((run.count,)),
            dma,
            dma((run.count,)),
        ]
    outs = (
        jax.ShapeDtypeStruct((1, z.orient, z.feat), F32),
        jax.ShapeDtypeStruct((1, z.orient), F32),
        jax.ShapeDtypeStruct((1, z.parts), F32),
    )
    parts = pl.pallas_call(
        functools.partial(kernel, z),
        out_shape=outs,
        in_specs=[hbm] * 7,
        out_specs=(vmem, vmem, vmem),
        scratch_shapes=[
            pltpu.VMEM((1, z.orient, z.feat), BF16),
            pltpu.VMEM((z.tiles, LANES), F32),
            pltpu.VMEM((2, LANES), jnp.int32),
            pltpu.SMEM((z.parts,), jnp.int32),
            pltpu.SMEM((z.parts,), jnp.int32),
            pltpu.VMEM((2, LANES), F32),
            pltpu.VMEM((2, z.parts, z.feat), BF16),
            pltpu.VMEM((2 * z.tiles * z.imgs, LANES), F32),
            pltpu.VMEM((z.tiles, LANES, 2 * LANES), BF16),
            pltpu.VMEM((2, z.parts, LANES), F32),
            pltpu.VMEM((z.rows, LANES), F32),
            pltpu.VMEM((z.refs, LANES), F32),
            pltpu.VMEM((z.imgs, LANES), F32),
            pltpu.VMEM((z.imgs, LANES), F32),
            pltpu.VMEM((z.group, 8, LANES), F32),
            pltpu.VMEM((z.imgs, LANES), F32),
            pltpu.VMEM((z.rows, LANES), BF16),
            pltpu.VMEM((z.refs, LANES), F32),
            dma,
            dma((6,)),
            dma((2,)),
            dma((2,)),
            dma,
            dma,
            *per_run,
        ],
        compiler_params=pltpu.CompilerParams(
            collective_id=0, has_side_effects=True, vmem_limit_bytes=64 * 2**20
        ),
        cost_estimate=pl.CostEstimate(
            flops=flops, bytes_accessed=4 * 2**20, transcendentals=z.rows * LANES
        ),
    )(
        particles,
        references,
        inv_noise.reshape(z.tiles, LANES),
        shifts.T,
        prior_class,
        prior_orient,
        circle,
    )
    bp, cw, ln = pl.pallas_call(
        finish,
        out_shape=outs,
        in_specs=[vmem] * 3,
        out_specs=(hbm,) * 3,
        scratch_shapes=[dma((3,))],
    )(*parts)
    return bp, cw, ln.reshape(z.parts)


def solution(mesh):
    def body(particles, references, inv_noise, shifts, prior_class, prior_orient):
        n_dom, n_cls = lax.axis_size("dom"), lax.axis_size("cls")
        z = Sizes(n_dom, n_cls, particles.shape[0], references.shape[1], particles.shape[1])
        return on_device(z, particles, references, inv_noise, shifts, prior_class, prior_orient)

    placed = (P("dom", None), P("dom", "cls", None), P(), P(), P("dom"), P("dom"))
    return jax.shard_map(
        body,
        mesh=mesh,
        in_specs=placed,
        out_specs=(P("dom", "cls", None), P("dom", "cls"), P("dom")),
        check_vma=False,
    )
```
